128 devices in a mesh: req: 16 (over y, x), head: 8 (over z, core).
Axes of the slice: x: 4, y: 4, z: 4, core: 2. Of those that a mesh axis runs over, the one named last changes fastest.
Arguments:
- hidden_in: bfloat16 [8192, 2048], P(('req', 'head')), may hold values from -6 to 6
- segment_ids: int32 [16, 512], P('req', 'head'), may hold values from 0 to 3, never falling along the last dimension, each value on 1 to 256 neighbouring positions
- attn_routes: int32 [8192, 2], P(('req', 'head')), may hold values from 0 to 7, all different within a row; in each aligned block of 512 rows (0 to 511, 512 to 1023, ...) at most 192 rows name the same one
- ffn_routes: int32 [8192, 2], P(('req', 'head')), may hold values from 0 to 7, all different within a row; in each aligned block of 64 rows (0 to 63, 64 to 127, ...) at most 24 rows name the same one
- attn_gain: float32 [2048], replicated, may hold values from 0.1 to 1.9
- attn_router: float32 [2048, 8], replicated, may hold values from -0.125 to 0.125
- w_query: bfloat16 [8, 2048, 2048], P(None, None, 'head'), may hold values from -1 to 1
- w_key: bfloat16 [2048, 2048], P(None, 'head'), may hold values from -32 to 32
- w_value: bfloat16 [2048, 2048], P(None, 'head'), may hold values from -0.125 to 0.125
- w_out: bfloat16 [8, 2048, 2048], P(None, 'head'), may hold values from -0.125 to 0.125
- ffn_gain: float32 [2048], replicated, may hold values from 0.1 to 1.9
- ffn_router: float32 [2048, 8], replicated, may hold values from -0.125 to 0.125
- w_gate_up: bfloat16 [8, 2048, 2, 5632], P('head', None, None, 'req'), may hold values from -0.125 to 0.125
- w_down: bfloat16 [8, 5632, 2048], P('head', 'req'), may hold values from -0.078125 to 0.078125
Outputs:
- layer_out: bfloat16 [8192, 2048], P(('req', 'head'))
The draws below stay inside these ranges and needn't reach their ends.
Inputs may be any that keep to these rules, and one draw needn't show every extreme that they name: `segment_ids`: within each row segment numbers never fall; each segment has 1 to 256 tokens. `attn_routes`: each token names two different experts; in each aligned block of 512 rows no expert is named by more than 192 rows. `ffn_routes`: each token names two different experts; in each aligned block of 64 rows (the rows of one device) no expert is named by more than 24 rows.
All inputs are finite; a program needn't handle non-finite values.
Results may differ from the reference program's by a relative error of at most 0.015.
Values may be sent and summed in bfloat16 or wider, within the bound.
No kernel may reach another device: no remote copies, remote signals or barrier semaphores. Data moves between devices by JAX's collectives and lax.ppermute only.
A program may use at most 128 MiB of HBM per device.

```python
import math
import jax
import jax.numpy as jnp
import numpy as np
from jax import lax

D = 2048
FF = 5632
H_KV = 16
HD = 128
E_ATT = 8
E_FF = 8
TOK_DEV = 64
TOK_REQ = 512
TOKENS = 8192
CAP_ATT = 192
C_FF = 24
N_REQ = 16
N_HEAD = 8


def paired_weights(random_key):
    base_key = jax.random.fold_in(random_key, 7)
    query_key, noise_key = jax.random.split(base_key, 2)
    queries = jnp.clip(jax.random.normal(query_key, (E_ATT, D, H_KV * HD), jnp.float32), -6.0, 6.0) * D ** (-0.5)
    noise = jnp.clip(jax.random.normal(noise_key, (D, H_KV * HD), jnp.float32), -6.0, 6.0) * D ** (-0.5)
    return (queries, noise)


def draw_w_query(key, part):
    queries, noise = paired_weights(key)
    return queries.astype(jnp.bfloat16)


def draw_w_key(key, part):
    queries, noise = paired_weights(key)
    return noise.astype(jnp.bfloat16)


def block_levels(stream_key, dims, cuts, smallest, high):
    level = 1.0
    for position, shards_of in cuts:
        heights = jax.random.uniform(jax.random.fold_in(jax.random.fold_in(stream_key, 6), position), (shards_of,), jnp.float32, smallest / len(cuts), high / len(cuts))
        level = level * jnp.repeat(jnp.exp(heights), dims[position] // shards_of).reshape((-1,) + (1,) * (len(dims) - 1 - position))
    return level


def split_up(count, total, reach, slope):
    weights = [(1 << 20) // math.isqrt(standing ** slope) + 1 for standing in range(2, count + 1)]
    surplus, holding = total - reach - (count - 1), [1] * (count - 1)
    while surplus > 0:
        free = [i for i in range(count - 1) if holding[i] < reach]
        mass, budget = sum([weights[i] for i in free]), surplus
        for i in free:
            addition = min(reach - holding[i], max(1, budget * weights[i] // mass), surplus)
            holding[i] = holding[i] + addition
            surplus = surplus - addition
    return np.array([reach] + holding)


def ragged_sizes(rng, amount, total, most, lean):
    if amount == 2:
        one = jax.random.randint(rng, (), max(1, total - most), min(most, total - 1) + 1)
        return jnp.stack([one, total - one])
    tallies = jnp.asarray(split_up(amount, total, most, lean), jnp.int32)
    pairs = (amount - 1) // 2
    source_of, receiver = tallies[1:1 + 2 * pairs:2], tallies[2:2 + 2 * pairs:2]
    room = jnp.minimum(source_of - 1, most - receiver)
    passed = jax.random.randint(jax.random.fold_in(rng, 1), (pairs,), 0, 1 << 20) % (room + 1)
    tallies = tallies.at[1:1 + 2 * pairs:2].set(source_of - passed).at[2:2 + 2 * pairs:2].set(receiver + passed)
    return tallies[jax.random.permutation(jax.random.fold_in(rng, 2), amount)]


def routed_block(key, own, number, rows, number_of, top, reach, slope):
    ranking = jax.random.permutation(key, number_of)
    heavy_load, usual = shares(number_of, rows * top, reach, slope, True), shares(number_of, rows * top, reach, slope, False)
    places = jnp.arange(number_of)

    def named(sizes, offset_by):
        used = int((sizes > 0).sum())
        fixed = max(1, used // 4)
        shifted = fixed + (places - fixed + offset_by * (used - fixed)) % max(1, number_of - fixed)
        return jnp.zeros((number_of,), jnp.int32).at[ranking[jnp.where(places < fixed, places, shifted)]].set(jnp.asarray(sizes, jnp.int32))

    sizes = jnp.where(number % 4 == 0, named(heavy_load, number // 4), named(usual, number - number // 4 - 1))
    mixed = jax.random.permutation(jax.random.fold_in(own, 3), number_of)
    source_of, receiver = mixed[0:number_of // 2 * 2:2], mixed[1:number_of // 2 * 2:2]
    slack = jnp.minimum(sizes[source_of] - 1, reach - sizes[receiver]) // 2
    slack = jnp.where((source_of == ranking[0]) | (receiver == ranking[0]) | (sizes[receiver] == 0), 0, jnp.maximum(slack, 0))
    shifted = jax.random.randint(jax.random.fold_in(own, 4), (number_of // 2,), 0, 1 << 20) % (slack + 1)
    sizes = sizes.at[source_of].add(-shifted).at[receiver].add(shifted)
    labels = jnp.searchsorted(jnp.cumsum(sizes), jnp.arange(rows * top), side="right").astype(jnp.int32)
    grid = labels.reshape(top, rows).T
    grid = grid[jax.random.permutation(jax.random.fold_in(own, 1), rows)]
    offset_by = jax.random.randint(jax.random.fold_in(own, 2), (rows, 1), 0, top)
    return jnp.take_along_axis(grid, (jnp.arange(top)[None, :] + offset_by) % top, axis=1)


def shares(count, total, reach, skew, full):
    weights = [(1 << 20) // math.isqrt(grade ** skew) + 1 for grade in range(1, count + 1)]
    largest = reach if full else min(reach, max(-(-total // count), total * weights[0] // sum(weights)))
    least = 1 if total - largest >= count - 1 else 0
    counts, rest = [largest] + [least] * (count - 1), total - largest - least * (count - 1)
    while rest > 0:
        movable = [i for i in range(1, count) if counts[i] < largest] or [i for i in range(1, count) if counts[i] < reach]
        pool, remaining = sum([weights[i] for i in movable]), rest
        for i in movable:
            more = min(reach - counts[i], max(1, remaining * weights[i] // pool), rest)
            counts[i] = counts[i] + more
            rest = rest - more
    return np.array(counts)


def gaussian(key, extent, spread, limit, cuts=(), held_as=jnp.bfloat16):
    drawn = jax.random.normal(key, extent, jnp.float32) * spread
    if len(cuts) > 0:
        drawn = block_levels(key, extent, cuts, -0.22, 0.18) * drawn
    return jnp.clip(drawn, min=-limit, max=limit).astype(held_as)


def setup_inputs(seed: int = 0) -> dict:
    splits = jax.random.split(jax.random.key(seed), 15)
    hidden_in = gaussian(splits[0], (TOKENS, D), 1.0, 6.0, ((0, 128),))
    segment_ids = jax.vmap(lambda own: jnp.searchsorted(jnp.cumsum(ragged_sizes(own, 4, TOK_REQ, TOK_REQ // 2, 2)), jnp.arange(TOK_REQ), side="right"))(jax.random.split(splits[1], N_REQ)).reshape((N_REQ, TOK_REQ)).astype(jnp.int32)
    attn_routes_keys = jax.random.split(jax.random.fold_in(splits[2], 1), TOKENS // TOK_REQ)
    attn_routes_turns = jax.random.permutation(jax.random.fold_in(splits[2], 3), TOKENS // TOK_REQ)
    attn_routes = jax.vmap(lambda own, number: routed_block(jax.random.fold_in(splits[2], 2), own, number, TOK_REQ, E_ATT, 2, CAP_ATT, 1))(attn_routes_keys, attn_routes_turns).reshape((TOKENS, 2))
    ffn_routes_keys = jax.random.split(jax.random.fold_in(splits[3], 1), TOKENS // TOK_DEV)
    ffn_routes_turns = jax.random.permutation(jax.random.fold_in(splits[3], 3), TOKENS // TOK_DEV)
    ffn_routes = jax.vmap(lambda own, number: routed_block(jax.random.fold_in(splits[3], 2), own, number, TOK_DEV, E_FF, 2, C_FF, 1))(ffn_routes_keys, ffn_routes_turns).reshape((TOKENS, 2))
    attn_gain = jnp.clip(1.0 + 0.18 * jax.random.normal(splits[4], (D,), jnp.float32), 0.1, 1.9)
    attn_router = gaussian(splits[5], (D, E_ATT), D ** -0.5, 0.125, (), jnp.float32)
    w_query = draw_w_query(jax.random.fold_in(splits[14], 71), 0)
    w_key = draw_w_key(jax.random.fold_in(splits[14], 71), 0)
    w_value = gaussian(splits[8], (D, H_KV * HD), D ** -0.5, 0.125, ((1, 8),))
    w_out = gaussian(splits[9], (E_ATT, H_KV * HD, D), (H_KV * HD) ** -0.5, 0.125, ((1, 8),))
    ffn_gain = jnp.clip(1.0 + 0.18 * jax.random.normal(splits[10], (D,), jnp.float32), 0.1, 1.9)
    ffn_router = gaussian(splits[11], (D, E_FF), D ** -0.5, 0.125, (), jnp.float32)
    w_gate_up = gaussian(splits[12], (E_FF, D, 2, FF), D ** -0.5, 0.125, ((0, 8), (3, 16)))
    w_down = gaussian(splits[13], (E_FF, FF, D), FF ** -0.5, 0.078125, ((0, 8), (1, 16)))
    return dict(hidden_in=hidden_in, segment_ids=segment_ids, attn_routes=attn_routes, ffn_routes=ffn_routes, attn_gain=attn_gain, attn_router=attn_router, w_query=w_query, w_key=w_key, w_value=w_value, w_out=w_out, ffn_gain=ffn_gain, ffn_router=ffn_router, w_gate_up=w_gate_up, w_down=w_down)


EPSILON = 1e-06
ROPE_BASE = 10000.0

def rms_norm(values, gain_vector):
    widened = values.astype(jnp.float32)
    inverse_rms = lax.rsqrt(lax.optimization_barrier(jnp.mean(widened * widened, axis=-1, keepdims=True)) + EPSILON)
    return (widened * inverse_rms * gain_vector).astype(jnp.bfloat16)

def pair_gates(normed, router, routes):
    logits = jnp.dot(normed.astype(jnp.float32), router, precision=lax.Precision.HIGHEST)
    picked = jnp.take_along_axis(logits, routes, axis=1)
    first_weight = jax.nn.sigmoid(picked[:, 0] - picked[:, 1])
    second_weight = jax.nn.sigmoid(picked[:, 1] - picked[:, 0])
    return jnp.stack([first_weight, second_weight], axis=1)

def positions(segment_row):
    earlier = (segment_row[None, :] < segment_row[:, None]).astype(jnp.int32)
    return (jnp.arange(segment_row.shape[0], dtype=jnp.int32) - lax.optimization_barrier(jnp.sum(earlier, axis=1))).astype(jnp.int32)

def rotary(values, token_place):
    half_width = values.shape[-1] // 2
    inverse = ROPE_BASE ** (-jnp.arange(half_width, dtype=jnp.float32) / half_width)
    shaped = token_place.astype(jnp.float32).reshape((-1,) + (1,) * (values.ndim - 2) + (1,))
    angles = shaped * inverse
    cosine = jnp.cos(angles)
    sines = jnp.sin(angles)
    lower_half = values[..., :half_width]
    upper_half = values[..., half_width:]
    return jnp.concatenate([lower_half * cosine - upper_half * sines, upper_half * cosine + lower_half * sines], axis=-1)

def slot_ranks(experts_flat, expert_count):
    onehot = (experts_flat[:, None] == jnp.arange(expert_count, dtype=jnp.int32)[None, :]).astype(jnp.int32)
    running = jnp.cumsum(onehot, axis=0) - onehot
    return lax.optimization_barrier(jnp.sum(running * onehot, axis=1)).astype(jnp.int32)

def soft_weights(scores, allowed):
    masked = jnp.where(allowed, scores, -1e+30)
    largest = lax.optimization_barrier(jnp.max(masked, axis=-1, keepdims=True))
    exponent = jnp.exp(masked - largest)
    return (exponent / lax.optimization_barrier(jnp.sum(exponent, axis=-1, keepdims=True))).astype(jnp.bfloat16)

def reference(hidden_in, segment_ids, attn_routes, ffn_routes, attn_gain, attn_router, w_query, w_key, w_value, w_out, ffn_gain, ffn_router, w_gate_up, w_down):
    seq_length = TOK_REQ
    capacity = CAP_ATT
    width = H_KV * HD
    normed = rms_norm(hidden_in, attn_gain)
    query_weights = w_query.astype(jnp.float32)
    out_weights = w_out.astype(jnp.float32)

    def attend_block(block_input):
        block_normed, segment_row, block_routes = block_input
        pair_weights = pair_gates(block_normed, attn_router, block_routes)
        token_place = positions(segment_row)
        flat_experts = block_routes.reshape(-1)
        slot_index = flat_experts * capacity + slot_ranks(flat_experts, E_ATT)
        slot_table = jnp.full((E_ATT * capacity,), 2 * seq_length, jnp.int32).at[slot_index].set(jnp.arange(2 * seq_length, dtype=jnp.int32))
        padded = jnp.concatenate([block_normed, jnp.zeros((1, D), jnp.bfloat16)], axis=0)
        buffer = padded[slot_table // 2].reshape(E_ATT, capacity, D)
        query_buf = jnp.einsum('ecd,edf->ecf', buffer.astype(jnp.float32), query_weights)
        queries = query_buf.reshape(E_ATT * capacity, width)[slot_index].reshape(seq_length, 2, H_KV, HD)
        queries = rotary(queries, token_place).astype(jnp.bfloat16)
        key_heads = jnp.dot(block_normed, w_key, preferred_element_type=jnp.float32).reshape(seq_length, H_KV, HD)
        key_heads = rotary(key_heads, token_place).astype(jnp.bfloat16)
        value_heads = jnp.dot(block_normed, w_value, preferred_element_type=jnp.float32).astype(jnp.bfloat16).reshape(seq_length, H_KV, HD)
        scores = jnp.einsum('tjhd,shd->hjts', queries.astype(jnp.float32), key_heads.astype(jnp.float32)) * HD ** (-0.5)
        indices = jnp.arange(seq_length, dtype=jnp.int32)
        allowed = (segment_row[:, None] == segment_row[None, :]) & (indices[None, :] <= indices[:, None])
        probs = soft_weights(scores, allowed)
        context = jnp.einsum('hjts,shd->tjhd', probs.astype(jnp.float32), value_heads.astype(jnp.float32)).astype(jnp.bfloat16)
        padded_ctx = jnp.concatenate([context.reshape(2 * seq_length, width), jnp.zeros((1, width), jnp.bfloat16)], axis=0)
        out_buf = padded_ctx[slot_table].reshape(E_ATT, capacity, width)
        projected = jnp.einsum('ecf,efd->ecd', out_buf.astype(jnp.float32), out_weights)
        per_pair = projected.reshape(E_ATT * capacity, D)[slot_index] * pair_weights.reshape(-1)[:, None]
        return lax.optimization_barrier(jnp.sum(per_pair.reshape(seq_length, 2, D), axis=1))
    attended = lax.map(attend_block, (normed.reshape(N_REQ, seq_length, D), segment_ids, attn_routes.reshape(N_REQ, seq_length, 2)))
    residual = (hidden_in.astype(jnp.float32) + attended.reshape(TOKENS, D)).astype(jnp.bfloat16)
    ffn_normed = rms_norm(residual, ffn_gain)
    ffn_weights = pair_gates(ffn_normed, ffn_router, ffn_routes)
    total_cap = N_REQ * N_HEAD * C_FF
    flat_experts = ffn_routes.reshape(-1)
    slot_index = flat_experts * total_cap + slot_ranks(flat_experts, E_FF)
    slot_table = jnp.full((E_FF * total_cap,), 2 * TOKENS, jnp.int32).at[slot_index].set(jnp.arange(2 * TOKENS, dtype=jnp.int32))
    padded = jnp.concatenate([ffn_normed, jnp.zeros((1, D), jnp.bfloat16)], axis=0)
    shard_width = FF // N_REQ

    def expert_block(expert_input):
        expert_table, gate_up, down_weights = expert_input
        rows_in = padded[expert_table // 2]
        gate_and_up = jnp.dot(rows_in, gate_up.reshape(D, 2 * FF), preferred_element_type=jnp.float32).reshape(total_cap, 2, FF)
        activation = (jax.nn.silu(gate_and_up[:, 0]) * gate_and_up[:, 1]).astype(jnp.bfloat16)
        shard_acts = activation.reshape(total_cap, N_REQ, shard_width).transpose(1, 0, 2)
        shard_downs = down_weights.reshape(N_REQ, shard_width, D)

        def add_shard(running_total, shard_input):
            act_shard, down_shard = shard_input
            partials = jnp.dot(act_shard, down_shard, preferred_element_type=jnp.float32).astype(jnp.bfloat16)
            return (running_total + lax.optimization_barrier(partials).astype(jnp.float32), jnp.zeros((), jnp.float32))
        summed, unused = lax.scan(add_shard, jnp.zeros((total_cap, D), jnp.float32), (shard_acts, shard_downs))
        return summed.astype(jnp.bfloat16)
    expert_out = lax.map(expert_block, (slot_table.reshape(E_FF, total_cap), w_gate_up, w_down))
    gathered = expert_out.reshape(E_FF * total_cap, D)[slot_index]
    mixture = lax.optimization_barrier(jnp.sum(gathered.astype(jnp.float32).reshape(TOKENS, 2, D) * ffn_weights[:, :, None], axis=1))
    return (residual.astype(jnp.float32) + mixture).astype(jnp.bfloat16)
```

```python
import functools

import jax
import jax.numpy as jnp
from jax import lax
from jax.experimental import pallas as pl
from jax.experimental.pallas import tpu as pltpu
from jax.sharding import PartitionSpec as P

D = 2048
HD = 128
META = 128
ROWS = 64
SEQ = 512
SLOTS = 24
HALF = 96
HID = 352
FF4 = 4 * HID
BF = jnp.bfloat16
F32 = jnp.float32
EPSILON = 1e-06
ROPE_BASE = 10000.0
AXES = ("req", "head")


def mate(v, parity):
    return v ^ 1 if parity == 0 else ((((v - 1) % 4) ^ 1) + 1) % 4


def square_perm(move_x, move_y, flip):
    pairs = []
    for i in range(128):
        r, h = divmod(i, 8)
        y, x = divmod(r, 4)
        parity = (h & 1) ^ flip
        ny = mate(y, parity) if move_y else y
        nx = mate(x, parity) if move_x else x
        pairs.append((i, (ny * 4 + nx) * 8 + h))
    return pairs


WX, WY = square_perm(1, 0, 0), square_perm(0, 1, 0)
TX, TY = square_perm(1, 0, 1), square_perm(0, 1, 1)
HA = [(h, h ^ (6 if h & 1 else 2)) for h in range(8)]
HB = [(h, h ^ (2 if h & 1 else 6)) for h in range(8)]
HC = [(h, h ^ 1) for h in range(8)]


def send_xy(v, pairs):
    return lax.ppermute(v, AXES, pairs)


def send_h(v, pairs):
    return lax.ppermute(v, "head", pairs)


def gather_head(own):
    a1 = send_h(own, HA)
    b1 = send_h(own, HB)
    c0 = send_h(own, HC)
    b2 = send_h(a1, HB)
    c1 = send_h(a1, HC)
    c2 = send_h(b1, HC)
    c3 = send_h(b2, HC)
    return [own, a1, b1, b2, c0, c1, c2, c3]


def mask_table():
    h = lax.axis_index("head").astype(jnp.int32)
    m_a = jnp.where(h & 1 == 0, 2, 6).astype(jnp.int32)
    m_b = 8 - m_a
    zero = jnp.zeros((), jnp.int32)
    gathered = [zero, m_a, m_b, zero + 4, zero + 1, m_b ^ 1, m_a ^ 1, zero + 5]
    scattered = [zero, m_b, m_a, zero + 4, zero + 1, m_a ^ 1, m_b ^ 1, zero + 5]
    return jnp.stack([h] + [h ^ m for m in gathered] + [h ^ m for m in scattered])


def split_router(router):
    hi = lax.reduce_precision(router, 8, 7)
    mid = lax.reduce_precision(router - hi, 8, 7)
    low = lax.reduce_precision(router - hi - mid, 8, 7)
    stacked = jnp.concatenate([hi, mid, low], axis=1).astype(BF)
    return jnp.pad(stacked, ((0, 0), (0, META - 24)))


def normalize(chunk, gain):
    wide = chunk.astype(F32)
    inverse = lax.rsqrt(jnp.mean(wide * wide, axis=-1, keepdims=True) + EPSILON)
    return (wide * inverse * gain).astype(BF)


def picked_gates(logits3, first, second):
    lane = lax.broadcasted_iota(jnp.int32, logits3.shape, 1)
    expert = (lane & 7).astype(F32)
    diff = jnp.where(expert == first, logits3, 0.0) - jnp.where(expert == second, logits3, 0.0)
    delta = jnp.sum(diff, axis=1, keepdims=True)
    return 1.0 / (1.0 + jnp.exp(-delta)), 1.0 / (1.0 + jnp.exp(delta))


def matmul(a, b):
    return jnp.dot(a, b, preferred_element_type=F32)


def matmul_t(a, b):
    return lax.dot_general(a, b, (((1,), (1,)), ((), ())), preferred_element_type=F32)


def attention_body(
    tab,
    c0, c1, c2, c3, c4, c5, c6, c7,
    gain, router, cos_t, sin_t, wq, wk, wv, wo,
    keep, send, sel,
    x_s, meta_s, q_s, k_s, v_s, rope_c, rope_s, gate_s, ctx_s, mix_s,
):
    step = pl.program_id(0)

    @pl.when(step == 0)
    def _():
        for i, ref in enumerate((c0, c1, c2, c3, c4, c5, c6, c7)):
            base = pl.multiple_of(tab[1 + i] * ROWS, ROWS)
            x_s[pl.ds(base, ROWS), :] = normalize(ref[:, :D], gain[...])
            meta_s[pl.ds(base, ROWS), :] = ref[:, D:].astype(F32)
        seg = meta_s[:, 0:1]
        cos_all = cos_t[...]
        sin_all = sin_t[...]
        c_sel = jnp.broadcast_to(cos_t[0:1, :], (SEQ, HD))
        s_sel = jnp.broadcast_to(sin_t[0:1, :], (SEQ, HD))
        for number in (1, 2, 3):
            start = jnp.sum(jnp.where(seg < float(number), 1.0, 0.0)).astype(jnp.int32)
            start = jnp.minimum(start, SEQ - 1)
            here = seg == float(number)
            c_sel = jnp.where(here, cos_t[pl.ds(start, 1), :], c_sel)
            s_sel = jnp.where(here, sin_t[pl.ds(start, 1), :], s_sel)
        lane = lax.broadcasted_iota(jnp.int32, (SEQ, HD), 1)
        rope_c[...] = cos_all * c_sel + sin_all * s_sel
        turned = sin_all * c_sel - cos_all * s_sel
        rope_s[...] = jnp.where(lane < HD // 2, -turned, turned)
        x = x_s[...]
        keys = matmul(x, wk[...])
        for g in range(2):
            one = keys[:, g * HD : (g + 1) * HD]
            k_s[:, g * HD : (g + 1) * HD] = (
                one * rope_c[...] + pltpu.roll(one, HD // 2, 1) * rope_s[...]
            ).astype(BF)
        v_s[...] = matmul(x, wv[...]).astype(BF)
        logits3 = matmul(x, router[...])
        g0, g1 = picked_gates(logits3, meta_s[:, 1:2], meta_s[:, 2:3])
        gate_s[:, 0:1] = g0
        gate_s[:, 1:2] = g1
        meta_row = jnp.transpose(meta_s[...])
        mine = tab[0].astype(F32)
        named = jnp.where((meta_row[3:4, :] == mine) | (meta_row[4:5, :] == mine), 1.0, 0.0)
        src = lax.broadcasted_iota(jnp.int32, (SEQ, SEQ), 0)
        dst = lax.broadcasted_iota(jnp.int32, (SEQ, SEQ), 1)
        earlier = jnp.where((src < dst) & (src // ROWS == dst // ROWS), 1.0, 0.0).astype(BF)
        rank = matmul(jnp.broadcast_to(named, (16, SEQ)).astype(BF), earlier)[0:1, :]
        token = lax.broadcasted_iota(jnp.int32, (1, SEQ), 1)
        slot = jnp.where(named > 0.5, rank.astype(jnp.int32) + (token // ROWS) * SLOTS, -1)
        rows = lax.broadcasted_iota(jnp.int32, (8 * SLOTS, SEQ), 0)
        sel[...] = jnp.where(rows == slot, 1.0, 0.0).astype(BF)

    @pl.when(step < 8)
    def _():
        here = step.astype(F32)
        query = matmul(x_s[...], wq[0])
        for j in range(2):
            chosen = meta_s[:, 1 + j : 2 + j] == here
            q_s[j] = jnp.where(chosen, query, q_s[j])

    @pl.when(step == 7)
    def _():
        seg_row = jnp.transpose(meta_s[...])[0:1, :]
        for g in range(2):
            cols = slice(g * HD, (g + 1) * HD)
            for block in range(4):
                lo = max(0, block * 128 - 256)
                hi = block * 128 + 128
                rows = slice(block * 128, hi)
                parts = []
                for j in range(2):
                    one = q_s[j, rows, cols]
                    parts.append(
                        (one * rope_c[rows, :] + pltpu.roll(one, HD // 2, 1) * rope_s[rows, :]).astype(BF)
                    )
                query = jnp.concatenate(parts, axis=0)
                scores = matmul_t(query, k_s[lo:hi, cols]) * HD ** (-0.5)
                q_pos = lax.broadcasted_iota(jnp.int32, (128, hi - lo), 0) + block * 128
                k_pos = lax.broadcasted_iota(jnp.int32, (128, hi - lo), 1) + lo
                allowed = (meta_s[rows, 0:1] == seg_row[:, lo:hi]) & (k_pos <= q_pos)
                allowed = jnp.concatenate([allowed.astype(F32)] * 2, axis=0) > 0.5
                masked = jnp.where(allowed, scores, -1e30)
                largest = jnp.max(masked, axis=-1, keepdims=True)
                exponent = jnp.exp(masked - largest)
                total = jnp.sum(exponent, axis=-1, keepdims=True)
                probs = (exponent / total).astype(BF)
                context = matmul(probs, v_s[lo:hi, cols])
                ctx_s[0, rows, cols] = context[:128]
                ctx_s[1, rows, cols] = context[128:]
        for i in range(8):
            base = pl.multiple_of(tab[9 + i] * ROWS, ROWS)
            take = pl.ds(base, ROWS)
            first = ctx_s[0, take, :].astype(BF).astype(F32) * gate_s[take, 0:1]
            second = ctx_s[1, take, :].astype(BF).astype(F32) * gate_s[take, 1:2]
            meta = meta_s[take, :]
            for e in range(8):
                mixed = jnp.where(meta[:, 1:2] == float(e), first, 0.0) + jnp.where(
                    meta[:, 2:3] == float(e), second, 0.0
                )
                mix_s[i * ROWS : (i + 1) * ROWS, e * 256 : (e + 1) * 256] = mixed.astype(BF)

    @pl.when(step >= 8)
    def _():
        weights = wo[...].reshape(8 * 256, 512)
        out = matmul(mix_s[...], weights)
        keep[...] = out[:256].astype(BF)
        send[...] = out[256:].astype(BF)


def attention(table, chunks, gain, router, cos_t, sin_t, w_query, w_key, w_value, w_out):
    whole = lambda shape: pl.BlockSpec(shape, lambda i, t: (0,) * len(shape))
    spec = pltpu.PrefetchScalarGridSpec(
        num_scalar_prefetch=1,
        grid=(12,),
        in_specs=[whole((ROWS, D + META))] * 8
        + [
            whole((1, D)),
            whole((D, META)),
            whole((SEQ, HD)),
            whole((SEQ, HD)),
            pl.BlockSpec((1, D, 256), lambda i, t: (jnp.minimum(i, 7), 0, 0)),
            whole((D, 256)),
            whole((D, 256)),
            pl.BlockSpec((8, 256, 512), lambda i, t: (0, 0, jnp.maximum(i - 8, 0))),
        ],
        out_specs=[
            pl.BlockSpec((256, 512), lambda i, t: (0, jnp.maximum(i - 8, 0))),
            pl.BlockSpec((256, 512), lambda i, t: (0, jnp.maximum(i - 8, 0))),
            whole((8 * SLOTS, SEQ)),
        ],
        scratch_shapes=[
            pltpu.VMEM((SEQ, D), BF),
            pltpu.VMEM((SEQ, META), F32),
            pltpu.VMEM((2, SEQ, 256), F32),
            pltpu.VMEM((SEQ, 256), BF),
            pltpu.VMEM((SEQ, 256), BF),
            pltpu.VMEM((SEQ, HD), F32),
            pltpu.VMEM((SEQ, HD), F32),
            pltpu.VMEM((SEQ, META), F32),
            pltpu.VMEM((2, SEQ, 256), F32),
            pltpu.VMEM((SEQ, 8 * 256), BF),
        ],
    )
    return pl.pallas_call(
        attention_body,
        grid_spec=spec,
        out_shape=[
            jax.ShapeDtypeStruct((256, D), BF),
            jax.ShapeDtypeStruct((256, D), BF),
            jax.ShapeDtypeStruct((8 * SLOTS, SEQ), BF),
        ],
        compiler_params=pltpu.CompilerParams(vmem_limit_bytes=56 << 20),
        name="attention",
    )(table, *chunks, gain, router, cos_t, sin_t, w_query, w_key, w_value, w_out)


def dispatch_body(tab, c0, c1, c2, c3, c4, c5, c6, c7, gain, sel, out_a, out_b, x_s):
    for i, ref in enumerate((c0, c1, c2, c3, c4, c5, c6, c7)):
        base = pl.multiple_of(tab[1 + i] * ROWS, ROWS)
        x_s[pl.ds(base, ROWS), :] = normalize(ref[...], gain[...])
    x = x_s[...]
    out_a[...] = matmul(sel[:HALF], x).astype(BF)
    out_b[...] = matmul(sel[HALF:], x).astype(BF)


def dispatch(table, chunks, gain, sel):
    vmem = pl.BlockSpec(memory_space=pltpu.VMEM)
    return pl.pallas_call(
        dispatch_body,
        in_specs=[pl.BlockSpec(memory_space=pltpu.SMEM)] + [vmem] * 10,
        out_specs=[vmem, vmem],
        out_shape=[jax.ShapeDtypeStruct((HALF, D), BF)] * 2,
        scratch_shapes=[pltpu.VMEM((SEQ, D), BF)],
        name="dispatch",
    )(table, *chunks, gain, sel)


def weigh_body(residual, gain, router, routes, high, low):
    normed = normalize(residual[...], gain[...])
    logits3 = matmul(normed, router[...])
    first = routes[:, 0:1]
    second = routes[:, 1:2]
    g0, g1 = picked_gates(logits3, first, second)
    lane = lax.broadcasted_iota(jnp.int32, (ROWS, META), 1).astype(F32)
    named = jnp.where((lane == first) | (lane == second), 1.0, 0.0)
    src = lax.broadcasted_iota(jnp.int32, (ROWS, ROWS), 1)
    dst = lax.broadcasted_iota(jnp.int32, (ROWS, ROWS), 0)
    earlier = jnp.where(src < dst, 1.0, 0.0).astype(BF)
    rank = matmul(earlier, named.astype(BF))
    rank0 = jnp.sum(jnp.where(lane == first, rank, 0.0), axis=1, keepdims=True)
    rank1 = jnp.sum(jnp.where(lane == second, rank, 0.0), axis=1, keepdims=True)
    column = lax.broadcasted_iota(jnp.int32, (ROWS, 8 * SLOTS), 1).astype(F32)
    table = jnp.where(column == first * SLOTS + rank0, g0, 0.0) + jnp.where(
        column == second * SLOTS + rank1, g1, 0.0
    )
    top = table.astype(BF)
    high[...] = top
    low[...] = (table - top.astype(F32)).astype(BF)


def weigh(residual, gain, router, routes):
    vmem = pl.BlockSpec(memory_space=pltpu.VMEM)
    return pl.pallas_call(
        weigh_body,
        in_specs=[vmem] * 4,
        out_specs=[vmem, vmem],
        out_shape=[jax.ShapeDtypeStruct((ROWS, 8 * SLOTS), BF)] * 2,
        name="weigh",
    )(residual, gain, router, routes)


def finish_body(residual, high, low, rows, out):
    values = rows[...]
    mixture = matmul(high[...], values) + matmul(low[...], values)
    out[...] = (residual[...].astype(F32) + mixture).astype(BF)


def finish(residual, high, low, rows):
    vmem = pl.BlockSpec(memory_space=pltpu.VMEM)
    return pl.pallas_call(
        finish_body,
        in_specs=[vmem] * 4,
        out_specs=vmem,
        out_shape=jax.ShapeDtypeStruct((ROWS, D), BF),
        name="finish",
    )(residual, high, low, rows)


def expert_body(sizes, outs, *refs):
    n = len(sizes)
    xs = refs[:n]
    gus = refs[n : n + 4]
    downs = refs[n + 4 : n + 8]
    out_refs = refs[n + 8 : n + 8 + len(outs)]
    wg, wu, wd, x_s, act_s, sems = refs[n + 8 + len(outs) :]
    copies = []
    for s in range(4):
        place = pl.ds(s * HID, HID)
        copies.append(
            (
                pltpu.make_async_copy(gus[s].at[0], wg.at[place, :], sems.at[0, s]),
                pltpu.make_async_copy(gus[s].at[1], wu.at[place, :], sems.at[1, s]),
                pltpu.make_async_copy(downs[s], wd.at[place, :], sems.at[2, s]),
            )
        )
    for s in range(4):
        copies[s][0].start()
        copies[s][1].start()
    for s in range(4):
        copies[s][2].start()
    row = 0
    for ref, size in zip(xs, sizes):
        x_s[row : row + size, :] = ref[...]
        row += size
    x = x_s[...]
    ready = 0
    for lo in range(0, FF4, 256):
        hi = min(lo + 256, FF4)
        while ready < 4 and ready * HID < hi:
            copies[ready][0].wait()
            copies[ready][1].wait()
            ready += 1
        gate = matmul_t(x, wg[lo:hi, :])
        up = matmul_t(x, wu[lo:hi, :])
        act_s[:, lo:hi] = (gate / (1.0 + jnp.exp(-gate)) * up).astype(BF)
    for s in range(4):
        copies[s][2].wait()
    act = act_s[...]
    for lo in range(0, D, 256):
        result = matmul(act, wd[:, lo : lo + 256]).astype(BF)
        row = 0
        for ref, size in zip(out_refs, outs):
            ref[:, lo : lo + 256] = result[row : row + size]
            row += size


def experts(xs, gus, downs, outs, name):
    sizes = tuple(x.shape[0] for x in xs)
    total = sum(sizes)
    vmem = pl.BlockSpec(memory_space=pltpu.VMEM)
    hbm = pl.BlockSpec(memory_space=pl.ANY)
    return pl.pallas_call(
        functools.partial(expert_body, sizes, outs),
        in_specs=[vmem] * len(xs) + [hbm] * 8,
        out_specs=[vmem] * len(outs),
        out_shape=[jax.ShapeDtypeStruct((size, D), BF) for size in outs],
        scratch_shapes=[
            pltpu.VMEM((FF4, D), BF),
            pltpu.VMEM((FF4, D), BF),
            pltpu.VMEM((FF4, D), BF),
            pltpu.VMEM((total, D), BF),
            pltpu.VMEM((total, FF4), BF),
            pltpu.SemaphoreType.DMA((3, 4)),
        ],
        compiler_params=pltpu.CompilerParams(vmem_limit_bytes=56 << 20),
        name=name,
    )(*xs, *gus, *downs)


def per_device(
    hidden_in,
    segment_ids,
    attn_routes,
    ffn_routes,
    attn_gain,
    attn_router,
    w_query,
    w_key,
    w_value,
    w_out,
    ffn_gain,
    ffn_router,
    w_gate_up,
    w_down,
):
    table = mask_table()
    gu = jnp.transpose(w_gate_up[0], (1, 2, 0))
    down = w_down[0]
    meta = jnp.concatenate([segment_ids.T, attn_routes, ffn_routes], axis=1).astype(BF)
    own = jnp.concatenate([hidden_in, jnp.pad(meta, ((0, 0), (0, META - 5)))], axis=1)
    chunks = gather_head(own)
    gu_x = send_xy(gu, WX)
    down_y = send_xy(down, WY)
    gu_y = send_xy(gu, WY)
    down_x = send_xy(down, WX)
    gu_d = send_xy(gu_x, WY)
    down_d = send_xy(down_y, WX)

    half = HD // 2
    inverse = ROPE_BASE ** (-jnp.arange(half, dtype=F32) / half)
    angles = jnp.arange(SEQ, dtype=F32)[:, None] * jnp.concatenate([inverse, inverse])[None, :]
    keep, send, sel = attention(
        table, chunks, attn_gain[None, :], split_router(attn_router), jnp.cos(angles), jnp.sin(angles),
        w_query, w_key, w_value, w_out,
    )
    got = send_h(send, HC)
    pass_a = (keep[128:].astype(F32) + got[128:].astype(F32)).astype(BF)
    got_a = send_h(pass_a, HA)
    held = keep[:128].astype(F32) + got[:128].astype(F32) + got_a.astype(F32)
    got_b = send_h(held[64:].astype(BF), HB)
    residual = (hidden_in.astype(F32) + held[:64] + got_b.astype(F32)).astype(BF)

    high, low = weigh(
        residual, ffn_gain[None, :], split_router(ffn_router),
        jnp.pad(ffn_routes.astype(F32), ((0, 0), (0, META - 2))),
    )
    x_a, x_b = dispatch(table, gather_head(residual), ffn_gain[None, :], sel)
    a_x = send_xy(x_a, TX)
    b_y = send_xy(x_b, TY)
    a_y = send_xy(x_a, TY)
    b_x = send_xy(x_b, TX)
    a_d = send_xy(a_x, TY)
    b_d = send_xy(b_y, TX)
    gus = (gu, gu_x, gu_y, gu_d)
    downs = (down, down_x, down_y, down_d)
    o_a, o_b, o_ax, o_by = experts((x_a, x_b, a_x, b_y), gus, downs, (HALF,) * 4, "experts_near")
    o_ay, o_bx = experts((a_y, a_d, b_x, b_d), gus, downs, (2 * HALF,) * 2, "experts_far")
    r_y = send_xy(o_ay, TY)
    r_x = send_xy(o_bx, TX)
    s_x = send_xy((o_ax.astype(F32) + r_y[HALF:].astype(F32)).astype(BF), TX)
    s_y = send_xy((o_by.astype(F32) + r_x[HALF:].astype(F32)).astype(BF), TY)
    rows_a = o_a.astype(F32) + r_y[:HALF].astype(F32) + s_x.astype(F32)
    rows_b = o_b.astype(F32) + r_x[:HALF].astype(F32) + s_y.astype(F32)
    rows = jnp.concatenate([rows_a, rows_b], axis=0).astype(BF).reshape(8, SLOTS, D)
    returned = lax.all_to_all(rows, "head", split_axis=0, concat_axis=0, tiled=True)
    return finish(residual, high, low, returned.reshape(8 * SLOTS, D))


def solution(mesh):
    return jax.shard_map(
        per_device,
        mesh=mesh,
        in_specs=(
            P(("req", "head"), None),
            P("req", "head"),
            P(("req", "head"), None),
            P(("req", "head"), None),
            P(),
            P(),
            P(None, None, "head"),
            P(None, "head"),
            P(None, "head"),
            P(None, "head", None),
            P(),
            P(),
            P("head", None, None, "req"),
            P("head", "req", None),
        ),
        out_specs=P(("req", "head"), None),
        check_vma=False,
    )
```

```python
import jax
import jax.numpy as jnp
from jax import lax
from jax.experimental import pallas as pl
from jax.experimental.pallas import tpu as pltpu
from jax.sharding import PartitionSpec as P


D = 2048
HD = 128
META = 128
ROWS = 64
SEQ = 512
SLOTS = 24
HID = 352
FF4 = 4 * HID
BF = jnp.bfloat16
F32 = jnp.float32
EPSILON = 1e-06
ROPE_BASE = 10000.0
AXES = ("req", "head")


def mate(v, parity):
    return v ^ 1 if parity == 0 else ((((v - 1) % 4) ^ 1) + 1) % 4


def square_perm(move_x, move_y, flip):
    pairs = []
    for i in range(128):
        r, h = divmod(i, 8)
        y, x = divmod(r, 4)
        parity = (h & 1) ^ flip
        ny = mate(y, parity) if move_y else y
        nx = mate(x, parity) if move_x else x
        pairs.append((i, (ny * 4 + nx) * 8 + h))
    return pairs


WX, WY = square_perm(1, 0, 0), square_perm(0, 1, 0)
TX, TY, TXY = square_perm(1, 0, 1), square_perm(0, 1, 1), square_perm(1, 1, 1)
HA = [(h, h ^ (6 if h & 1 else 2)) for h in range(8)]
HB = [(h, h ^ (2 if h & 1 else 6)) for h in range(8)]
HC = [(h, h ^ 1) for h in range(8)]


def send_xy(v, pairs):
    return lax.ppermute(v, AXES, pairs)


def send_h(v, pairs):
    return lax.ppermute(v, "head", pairs)


def gather_head(own):
    a1 = send_h(own, HA)
    b1 = send_h(own, HB)
    c0 = send_h(own, HC)
    b2 = send_h(a1, HB)
    c1 = send_h(a1, HC)
    c2 = send_h(b1, HC)
    c3 = send_h(b2, HC)
    return [own, a1, b1, b2, c0, c1, c2, c3]


def head_order(scatter):
    h = lax.axis_index("head")
    m_a = 2 + 4 * (h & 1)
    m_b = 8 - m_a
    if scatter:
        m_a, m_b = m_b, m_a
        masks = (0, m_a, m_b, 4, 1, m_b ^ 1, m_a ^ 1, 5)
    else:
        masks = (0, m_a, m_b, 4, 1, m_b ^ 1, m_a ^ 1, 5)
    return [h ^ m for m in masks]


def split_router(router):
    hi = router.astype(BF).astype(F32)
    mid = (router - hi).astype(BF).astype(F32)
    low = router - hi - mid
    return jnp.concatenate([hi, mid, low, jnp.zeros_like(low)], axis=0).astype(BF)


def normalize(chunk, gain):
    wide = chunk.astype(F32)
    inverse = lax.rsqrt(jnp.mean(wide * wide, axis=-1, keepdims=True) + EPSILON)
    return (wide * inverse * gain).astype(BF)


def picked_gates(logits3, first, second):
    lane = lax.broadcasted_iota(jnp.int32, logits3.shape, 1)
    expert = (lane & 7).astype(F32)
    diff = jnp.where(expert == first, logits3, 0.0) - jnp.where(expert == second, logits3, 0.0)
    delta = jnp.sum(diff, axis=1, keepdims=True)
    return 1.0 / (1.0 + jnp.exp(-delta)), 1.0 / (1.0 + jnp.exp(delta))


def matmul(a, b):
    return jnp.dot(a, b, preferred_element_type=F32)


def matmul_t(a, b):
    return lax.dot_general(a, b, (((1,), (1,)), ((), ())), preferred_element_type=F32)


def attention_body(
    c0, c1, c2, c3, c4, c5, c6, c7,
    gain, router, cos_t, sin_t, wq, wk, wv, wo,
    keep, send,
    x_s, meta_s, q_s, k_s, v_s, rope_c, rope_s, gate_s, ctx_s, mix_s,
):
    step = pl.program_id(0)

    @pl.when(step == 0)
    def _():
        for place, ref in zip(head_order(False), (c0, c1, c2, c3, c4, c5, c6, c7)):
            base = pl.multiple_of(place * ROWS, ROWS)
            x_s[pl.ds(base, ROWS), :] = normalize(ref[:, :D], gain[...])
            meta_s[pl.ds(base, ROWS), :] = ref[:, D:].astype(F32)
        seg = meta_s[:, 0:1]
        cos_all = cos_t[...]
        sin_all = sin_t[...]
        c_sel = jnp.broadcast_to(cos_t[0:1, :], (SEQ, HD))
        s_sel = jnp.broadcast_to(sin_t[0:1, :], (SEQ, HD))
        for number in (1, 2, 3):
            start = jnp.sum(jnp.where(seg < float(number), 1.0, 0.0)).astype(jnp.int32)
            start = jnp.minimum(start, SEQ - 1)
            here = seg == float(number)
            c_sel = jnp.where(here, cos_t[pl.ds(start, 1), :], c_sel)
            s_sel = jnp.where(here, sin_t[pl.ds(start, 1), :], s_sel)
        lane = lax.broadcasted_iota(jnp.int32, (SEQ, HD), 1)
        rope_c[...] = cos_all * c_sel + sin_all * s_sel
        turned = sin_all * c_sel - cos_all * s_sel
        rope_s[...] = jnp.where(lane < HD // 2, -turned, turned)
        x = x_s[...]
        keys = matmul(x, wk[...])
        for g in range(2):
            one = keys[:, g * HD : (g + 1) * HD]
            k_s[:, g * HD : (g + 1) * HD] = (
                one * rope_c[...] + pltpu.roll(one, HD // 2, 1) * rope_s[...]
            ).astype(BF)
        v_s[...] = matmul(x, wv[...]).astype(BF)
        logits3 = matmul_t(x, split_router(router[...]))
        g0, g1 = picked_gates(logits3, meta_s[:, 1:2], meta_s[:, 2:3])
        gate_s[:, 0:1] = g0
        gate_s[:, 1:2] = g1

    @pl.when(step < 8)
    def _():
        here = step.astype(F32)
        query = matmul(x_s[...], wq[0])
        for j in range(2):
            chosen = meta_s[:, 1 + j : 2 + j] == here
            q_s[j] = jnp.where(chosen, query, q_s[j])

    @pl.when(step == 7)
    def _():
        seg_row = jnp.transpose(meta_s[...])[0:1, :]
        for g in range(2):
            cols = slice(g * HD, (g + 1) * HD)
            for block in range(4):
                lo = max(0, block * 128 - 256)
                hi = block * 128 + 128
                rows = slice(block * 128, hi)
                parts = []
                for j in range(2):
                    one = q_s[j, rows, cols]
                    parts.append(
                        (one * rope_c[rows, :] + pltpu.roll(one, HD // 2, 1) * rope_s[rows, :]).astype(BF)
                    )
                query = jnp.concatenate(parts, axis=0)
                scores = matmul_t(query, k_s[lo:hi, cols]) * HD ** (-0.5)
                q_pos = lax.broadcasted_iota(jnp.int32, (128, hi - lo), 0) + block * 128
                k_pos = lax.broadcasted_iota(jnp.int32, (128, hi - lo), 1) + lo
                allowed = (meta_s[rows, 0:1] == seg_row[:, lo:hi]) & (k_pos <= q_pos)
                allowed = jnp.concatenate([allowed.astype(F32)] * 2, axis=0) > 0.5
                masked = jnp.where(allowed, scores, -1e30)
                largest = jnp.max(masked, axis=-1, keepdims=True)
                exponent = jnp.exp(masked - largest)
                total = jnp.sum(exponent, axis=-1, keepdims=True)
                probs = (exponent / total).astype(BF)
                context = matmul(probs, v_s[lo:hi, cols])
                ctx_s[0, rows, cols] = context[:128]
                ctx_s[1, rows, cols] = context[128:]
        for i, place in enumerate(head_order(True)):
            base = pl.multiple_of(place * ROWS, ROWS)
            take = pl.ds(base, ROWS)
            first = ctx_s[0, take, :].astype(BF).astype(F32) * gate_s[take, 0:1]
            second = ctx_s[1, take, :].astype(BF).astype(F32) * gate_s[take, 1:2]
            meta = meta_s[take, :]
            for e in range(8):
                mixed = jnp.where(meta[:, 1:2] == float(e), first, 0.0) + jnp.where(
                    meta[:, 2:3] == float(e), second, 0.0
                )
                mix_s[i * ROWS : (i + 1) * ROWS, e * 256 : (e + 1) * 256] = mixed.astype(BF)

    @pl.when(step >= 8)
    def _():
        weights = wo[...].reshape(8 * 256, 512)
        out = matmul(mix_s[...], weights)
        keep[...] = out[:256].astype(BF)
        send[...] = out[256:].astype(BF)


def attention(chunks, gain, router, cos_t, sin_t, w_query, w_key, w_value, w_out):
    whole = lambda shape: pl.BlockSpec(shape, lambda i: (0,) * len(shape))
    spec = pltpu.PrefetchScalarGridSpec(
        num_scalar_prefetch=0,
        grid=(12,),
        in_specs=[whole((ROWS, D + META))] * 8
        + [
            whole((1, D)),
            whole((8, D)),
            whole((SEQ, HD)),
            whole((SEQ, HD)),
            pl.BlockSpec((1, D, 256), lambda i: (jnp.minimum(i, 7), 0, 0)),
            whole((D, 256)),
            whole((D, 256)),
            pl.BlockSpec((8, 256, 512), lambda i: (0, 0, jnp.maximum(i - 8, 0))),
        ],
        out_specs=[
            pl.BlockSpec((256, 512), lambda i: (0, jnp.maximum(i - 8, 0))),
            pl.BlockSpec((256, 512), lambda i: (0, jnp.maximum(i - 8, 0))),
        ],
        scratch_shapes=[
            pltpu.VMEM((SEQ, D), BF),
            pltpu.VMEM((SEQ, META), F32),
            pltpu.VMEM((2, SEQ, 256), F32),
            pltpu.VMEM((SEQ, 256), BF),
            pltpu.VMEM((SEQ, 256), BF),
            pltpu.VMEM((SEQ, HD), F32),
            pltpu.VMEM((SEQ, HD), F32),
            pltpu.VMEM((SEQ, META), F32),
            pltpu.VMEM((2, SEQ, 256), F32),
            pltpu.VMEM((SEQ, 8 * 256), BF),
        ],
    )
    return pl.pallas_call(
        attention_body,
        grid_spec=spec,
        out_shape=[
            jax.ShapeDtypeStruct((256, D), BF),
            jax.ShapeDtypeStruct((256, D), BF),
        ],
        compiler_params=pltpu.CompilerParams(vmem_limit_bytes=40 << 20),
        name="attention",
    )(*chunks, gain, router, cos_t, sin_t, w_query, w_key, w_value, w_out)


def prepare_body(hidden, segments, routes, out):
    out[:, :D] = hidden[...]
    rows = jnp.concatenate([segments[...], routes[...], jnp.zeros((5, ROWS), jnp.int32)], axis=0).astype(F32)
    rows = jnp.concatenate([rows, jnp.zeros((META - 8, ROWS), F32)], axis=0)
    out[:, D:] = jnp.transpose(rows).astype(BF)


def prepare(hidden, segments, routes):
    vmem = pl.BlockSpec(memory_space=pltpu.VMEM)
    return pl.pallas_call(
        prepare_body,
        in_specs=[vmem] * 3,
        out_specs=vmem,
        out_shape=jax.ShapeDtypeStruct((ROWS, D + META), BF),
        compiler_params=pltpu.CompilerParams(vmem_limit_bytes=8 << 20),
        name="prepare",
    )(hidden, segments, routes)


def slot_rows(routes):
    first = routes[0:1, :]
    second = routes[1:2, :]
    expert = lax.broadcasted_iota(jnp.int32, (16, ROWS), 0)
    named = jnp.where((expert == first) | (expert == second), 1.0, 0.0)
    src = lax.broadcasted_iota(jnp.int32, (ROWS, ROWS), 0)
    dst = lax.broadcasted_iota(jnp.int32, (ROWS, ROWS), 1)
    rank = matmul(named.astype(BF), jnp.where(src < dst, 1.0, 0.0).astype(BF)).astype(jnp.int32)
    rank0 = jnp.sum(jnp.where(expert == first, rank, 0), axis=0, keepdims=True)
    rank1 = jnp.sum(jnp.where(expert == second, rank, 0), axis=0, keepdims=True)
    return first * SLOTS + rank0, second * SLOTS + rank1


def settle_body(hidden, keep, got, got_a, got_b, gain, routes, residual, rows):
    total = keep[:ROWS].astype(F32) + got[:ROWS].astype(F32) + got_a[:ROWS].astype(F32) + got_b[...].astype(F32)
    value = (hidden[...].astype(F32) + total).astype(BF)
    residual[...] = value
    normed = normalize(value, gain[...])
    slot0, slot1 = slot_rows(routes[...])
    row = lax.broadcasted_iota(jnp.int32, (8 * SLOTS, ROWS), 0)
    pick = jnp.where((row == slot0) | (row == slot1), 1.0, 0.0).astype(BF)
    rows[...] = matmul(pick, normed).astype(BF)


def settle(hidden, keep, got, got_a, got_b, gain, routes):
    vmem = pl.BlockSpec(memory_space=pltpu.VMEM)
    part = lambda n: pl.BlockSpec((n, D), lambda i: (0, 0))
    full = lambda shape: pl.BlockSpec(shape, lambda i: (0, 0))
    return pl.pallas_call(
        settle_body,
        grid=(1,),
        in_specs=[part(ROWS)] * 5 + [full((1, D)), full((2, ROWS))],
        out_specs=[part(ROWS), part(8 * SLOTS)],
        out_shape=[jax.ShapeDtypeStruct((ROWS, D), BF), jax.ShapeDtypeStruct((8 * SLOTS, D), BF)],
        compiler_params=pltpu.CompilerParams(vmem_limit_bytes=8 << 20),
        name="settle",
    )(hidden, keep, got, got_a, got_b, gain, routes)


def weigh_body(residual, gain, router, routes, high, low):
    normed = normalize(residual[...], gain[...])
    split = matmul_t(split_router(router[...]), normed)
    logits = split[0:8] + split[8:16] + split[16:24]
    expert = lax.broadcasted_iota(jnp.int32, (8, ROWS), 0)
    picked = routes[...]
    one = jnp.sum(jnp.where(expert == picked[0:1], logits, 0.0), axis=0, keepdims=True)
    two = jnp.sum(jnp.where(expert == picked[1:2], logits, 0.0), axis=0, keepdims=True)
    slot0, slot1 = slot_rows(picked)
    row = lax.broadcasted_iota(jnp.int32, (8 * SLOTS, ROWS), 0)
    table = jnp.where(row == slot0, 1.0 / (1.0 + jnp.exp(two - one)), 0.0) + jnp.where(
        row == slot1, 1.0 / (1.0 + jnp.exp(one - two)), 0.0
    )
    top = table.astype(BF)
    high[...] = top
    low[...] = (table - top.astype(F32)).astype(BF)


def weigh(residual, gain, router, routes):
    vmem = pl.BlockSpec(memory_space=pltpu.VMEM)
    return pl.pallas_call(
        weigh_body,
        in_specs=[vmem] * 4,
        out_specs=[vmem, vmem],
        out_shape=[jax.ShapeDtypeStruct((8 * SLOTS, ROWS), BF)] * 2,
        compiler_params=pltpu.CompilerParams(vmem_limit_bytes=8 << 20),
        name="weigh",
    )(residual, gain, router, routes)


def finish_body(residual, high, low, rows, out):
    values = rows[...]
    first_dim = (((0,), (0,)), ((), ()))
    mixture = lax.dot_general(high[...], values, first_dim, preferred_element_type=F32)
    mixture = mixture + lax.dot_general(low[...], values, first_dim, preferred_element_type=F32)
    out[...] = (residual[...].astype(F32) + mixture).astype(BF)


def finish(residual, high, low, rows):
    vmem = pl.BlockSpec(memory_space=pltpu.VMEM)
    return pl.pallas_call(
        finish_body,
        in_specs=[vmem] * 4,
        out_specs=vmem,
        out_shape=jax.ShapeDtypeStruct((ROWS, D), BF),
        compiler_params=pltpu.CompilerParams(vmem_limit_bytes=8 << 20),
        name="finish",
    )(residual, high, low, rows)


def pack_body(*refs):
    out, sems = refs[8], refs[9]
    copies = []
    for s in range(4):
        for part in range(3):
            src = refs[s].at[part] if part < 2 else refs[4 + s]
            place = pl.ds(part * FF4 + s * HID, HID)
            copies.append(pltpu.make_async_copy(src, out.at[place, :], sems.at[part, s]))
    for copy in copies:
        copy.start()
    for copy in copies:
        copy.wait()


def pack(gus, downs):
    hbm = pl.BlockSpec(memory_space=pl.ANY)
    return pl.pallas_call(
        pack_body,
        in_specs=[hbm] * 8,
        out_specs=pl.BlockSpec(memory_space=pltpu.VMEM),
        out_shape=pltpu.VMEM((3 * FF4, D), BF),
        scratch_shapes=[pltpu.SemaphoreType.DMA((3, 4))],
        compiler_params=pltpu.CompilerParams(vmem_limit_bytes=4 << 20),
        name="pack",
    )(*gus, *downs)


def expert_body(rows, weights, out, act_s):
    x = rows[...]
    for lo in range(0, FF4, 256):
        hi = min(lo + 256, FF4)
        gate = matmul_t(x, weights[lo:hi, :])
        up = matmul_t(x, weights[FF4 + lo : FF4 + hi, :])
        act_s[:, lo:hi] = (gate / (1.0 + jnp.exp(-gate)) * up).astype(BF)
    act = act_s[...]
    for lo in range(0, D, 256):
        out[:, lo : lo + 256] = matmul(act, weights[2 * FF4 :, lo : lo + 256]).astype(BF)


def experts(rows, weights):
    vmem = pl.BlockSpec(memory_space=pltpu.VMEM)
    return pl.pallas_call(
        expert_body,
        in_specs=[vmem] * 2,
        out_specs=vmem,
        out_shape=jax.ShapeDtypeStruct(rows.shape, BF),
        scratch_shapes=[pltpu.VMEM((rows.shape[0], FF4), BF)],
        compiler_params=pltpu.CompilerParams(vmem_limit_bytes=8 << 20),
    )(rows, weights)


def per_device(
    hidden_in,
    segment_ids,
    attn_routes,
    ffn_routes,
    attn_gain,
    attn_router,
    w_query,
    w_key,
    w_value,
    w_out,
    ffn_gain,
    ffn_router,
    w_gate_up,
    w_down,
):
    gu = jnp.transpose(w_gate_up[0], (1, 2, 0))
    down = w_down[0]
    own = prepare(hidden_in, segment_ids, attn_routes.T)
    chunks = gather_head(own)
    gu_x = send_xy(gu, WX)
    down_y = send_xy(down, WY)
    gu_y = send_xy(gu, WY)
    down_x = send_xy(down, WX)
    gu_d = send_xy(gu_x, WY)
    down_d = send_xy(down_y, WX)

    half = HD // 2
    inverse = ROPE_BASE ** (-jnp.arange(half, dtype=F32) / half)
    angles = jnp.arange(SEQ, dtype=F32)[:, None] * jnp.concatenate([inverse, inverse])[None, :]
    cosine, sine = jnp.cos(angles), jnp.sin(angles)
    keep, send = attention(
        chunks, attn_gain[None, :], attn_router.T, cosine, sine, w_query, w_key, w_value, w_out
    )
    got = send_h(send, HC)
    pass_a = (keep[128:].astype(F32) + got[128:].astype(F32)).astype(BF)
    got_a = send_h(pass_a, HA)
    held = keep[64:128].astype(F32) + got[64:128].astype(F32) + got_a[64:].astype(F32)
    got_b = send_h(held.astype(BF), HB)
    residual, rows = settle(hidden_in, keep, got, got_a, got_b, ffn_gain[None, :], ffn_routes.T)
    arrived = lax.all_to_all(rows.reshape(8, SLOTS, D), "head", split_axis=0, concat_axis=0, tiled=True)
    high, low = weigh(residual, ffn_gain[None, :], ffn_router.T, ffn_routes.T)
    x_own = arrived.reshape(8 * SLOTS, D)
    weights = pack((gu, gu_x, gu_y, gu_d), (down, down_x, down_y, down_d))
    x_d = send_xy(x_own, TXY)
    x_x = send_xy(x_own, TX)
    x_y = send_xy(x_own, TY)
    part = experts(x_own, weights)
    part_d = experts(x_d, weights)
    got_d = send_xy(part_d, TXY)
    part_x = experts(x_x, weights)
    got_x = send_xy(part_x, TX)
    part_y = experts(x_y, weights)
    got_y = send_xy(part_y, TY)
    rows = part.astype(F32) + got_d.astype(F32) + got_x.astype(F32) + got_y.astype(F32)
    rows = rows.astype(BF).reshape(8, SLOTS, D)
    returned = lax.all_to_all(rows, "head", split_axis=0, concat_axis=0, tiled=True)
    return finish(residual, high, low, returned.reshape(8 * SLOTS, D))


def solution(mesh):
    return jax.shard_map(
        per_device,
        mesh=mesh,
        in_specs=(
            P(("req", "head"), None),
            P("req", "head"),
            P(("req", "head"), None),
            P(("req", "head"), None),
            P(),
            P(),
            P(None, None, "head"),
            P(None, "head"),
            P(None, "head"),
            P(None, "head", None),
            P(),
            P(),
            P("head", None, None, "req"),
            P("head", "req", None),
        ),
        out_specs=P(("req", "head"), None),
        check_vma=False,
    )
```

```python
import math

import jax
import jax.numpy as jnp
from jax import lax
from jax.experimental import pallas as pl
from jax.experimental.pallas import tpu as pltpu
from jax.sharding import PartitionSpec as P


D = 2048
HD = 128
META = 128
ROWS = 64
SEQ = 512
SLOTS = 24
HID = 352
FF4 = 4 * HID
CUT = 3 * HID // 2
BF = jnp.bfloat16
F32 = jnp.float32
EPSILON = 1e-06
ROPE_BASE = 10000.0
SOFTMAX_SCALE = HD ** (-0.5) * math.log2(math.e)
AXES = ("req", "head")


def mate(v, parity):
    return v ^ 1 if parity == 0 else ((((v - 1) % 4) ^ 1) + 1) % 4


def square_perm(move_x, move_y, flip):
    pairs = []
    for i in range(128):
        r, h = divmod(i, 8)
        y, x = divmod(r, 4)
        parity = (h & 1) ^ flip
        ny = mate(y, parity ^ 1) if move_y else y
        nx = mate(x, parity) if move_x else x
        pairs.append((i, (ny * 4 + nx) * 8 + h))
    return pairs


WX, WY = square_perm(1, 0, 0), square_perm(0, 1, 0)
TX, TY, TXY = square_perm(1, 0, 1), square_perm(0, 1, 1), square_perm(1, 1, 1)
HA = [(h, h ^ (6 if h & 1 else 2)) for h in range(8)]
HB = [(h, h ^ (2 if h & 1 else 6)) for h in range(8)]
HC = [(h, h ^ 1) for h in range(8)]


def send_xy(v, pairs):
    return lax.ppermute(v, AXES, pairs)


def send_h(v, pairs):
    return lax.ppermute(v, "head", pairs)


def gather_head(own):
    a1 = send_h(own, HA)
    b1 = send_h(own, HB)
    c0 = send_h(own, HC)
    b2 = send_h(a1, HB)
    c1 = send_h(a1, HC)
    c2 = send_h(b1, HC)
    c3 = send_h(b2, HC)
    return [own, a1, b1, b2, c0, c1, c2, c3]


def head_order(scatter):
    h = lax.axis_index("head")
    m_a = 2 + 4 * (h & 1)
    m_b = 8 - m_a
    if scatter:
        m_a, m_b = m_b, m_a
        masks = (0, m_a, m_b, 4, 1, m_b ^ 1, m_a ^ 1, 5)
    else:
        masks = (0, m_a, m_b, 4, 1, m_b ^ 1, m_a ^ 1, 5)
    return [h ^ m for m in masks]


def split_router(router):
    hi = router.astype(BF).astype(F32)
    mid = (router - hi).astype(BF).astype(F32)
    low = router - hi - mid
    return jnp.concatenate([hi, mid, low, jnp.zeros_like(low)], axis=0).astype(BF)


def normalize(chunk, gain):
    wide = chunk.astype(F32)
    inverse = lax.rsqrt(jnp.mean(wide * wide, axis=-1, keepdims=True) + EPSILON)
    return (wide * inverse * gain).astype(BF)


def picked_gates(logits3, first, second):
    lane = lax.broadcasted_iota(jnp.int32, logits3.shape, 1)
    expert = (lane & 7).astype(F32)
    diff = jnp.where(expert == first, logits3, 0.0) - jnp.where(expert == second, logits3, 0.0)
    delta = jnp.sum(diff, axis=1, keepdims=True)
    return 1.0 / (1.0 + jnp.exp(-delta)), 1.0 / (1.0 + jnp.exp(delta))


def matmul(a, b):
    return jnp.dot(a, b, preferred_element_type=F32)


def matmul_t(a, b):
    return lax.dot_general(a, b, (((1,), (1,)), ((), ())), preferred_element_type=F32)


def attention_body(
    c0, c1, c2, c3, c4, c5, c6, c7,
    router, cos_t, sin_t, wq, wk, wv, wo,
    keep, send,
    x_s, meta_s, named_s, q_s, k_s, v_s, rope_c, rope_s, gate_s, ctx_s, mix_s, wq_s, kv_w, wo_s, sems,
):
    query_copies = [
        pltpu.make_async_copy(wq.at[e], wq_s.at[:, pl.ds(e * 256, 256)], sems.at[e]) for e in range(8)
    ]
    key_copy = pltpu.make_async_copy(wk, kv_w.at[:, pl.ds(0, 256)], sems.at[8])
    value_copy = pltpu.make_async_copy(wv, kv_w.at[:, pl.ds(256, 256)], sems.at[9])
    out_copy = pltpu.make_async_copy(wo, wo_s, sems.at[10])
    key_copy.start()
    value_copy.start()
    for copy in query_copies:
        copy.start()
    out_copy.start()

    for place, ref in zip(head_order(False), (c0, c1, c2, c3, c4, c5, c6, c7)):
        base = pl.multiple_of(place * ROWS, ROWS)
        x_s[pl.ds(base, ROWS), :] = ref[:, :D]
        meta_s[pl.ds(base, ROWS), :] = ref[:, D:].astype(F32)
    seg = meta_s[:, 0:1]
    for j in range(2):
        named_s[j] = jnp.broadcast_to(meta_s[:, 1 + j : 2 + j], (SEQ, HD))
    cos_all = cos_t[...]
    sin_all = sin_t[...]
    c_sel = jnp.broadcast_to(cos_t[0:1, :], (SEQ, HD))
    s_sel = jnp.broadcast_to(sin_t[0:1, :], (SEQ, HD))
    for number in (1, 2, 3):
        start = jnp.sum(jnp.where(seg < float(number), 1.0, 0.0)).astype(jnp.int32)
        start = jnp.minimum(start, SEQ - 1)
        here = seg == float(number)
        c_sel = jnp.where(here, cos_t[pl.ds(start, 1), :], c_sel)
        s_sel = jnp.where(here, sin_t[pl.ds(start, 1), :], s_sel)
    lane = lax.broadcasted_iota(jnp.int32, (SEQ, HD), 1)
    rope_c[...] = cos_all * c_sel + sin_all * s_sel
    turned = sin_all * c_sel - cos_all * s_sel
    rope_s[...] = jnp.where(lane < HD // 2, -turned, turned)
    logits3 = matmul_t(x_s[...], split_router(router[...]))
    g0, g1 = picked_gates(logits3, meta_s[:, 1:2], meta_s[:, 2:3])
    gate_s[:, 0:1] = g0
    gate_s[:, 1:2] = g1
    key_copy.wait()
    value_copy.wait()
    both = matmul(x_s[...], kv_w[...])
    v_s[...] = both[:, 256:].astype(BF)
    for g in range(2):
        one = both[:, g * HD : (g + 1) * HD]
        k_s[:, g * HD : (g + 1) * HD] = (
            one * rope_c[...] + pltpu.roll(one, HD // 2, 1) * rope_s[...]
        ).astype(BF)
    for copy in query_copies:
        copy.wait()

    def query_step(pair, carry):
        here = (2 * pair).astype(F32)
        query = matmul(x_s[...], wq_s[:, pl.ds(pl.multiple_of(pair * 512, 512), 512)])
        for j in range(2):
            is_first = named_s[j] == here
            is_second = named_s[j] == here + 1.0
            for g in range(2):
                cols = slice(g * HD, (g + 1) * HD)
                other = query[:, 256 + g * HD : 256 + (g + 1) * HD]
                q_s[j, :, cols] = jnp.where(
                    is_first, query[:, cols], jnp.where(is_second, other, q_s[j, :, cols])
                )
        return carry

    lax.fori_loop(0, 4, query_step, 0)
    seg_row = jnp.transpose(meta_s[...])[0:1, :]
    for block in range(4):
        lo = max(0, block * 128 - 256)
        hi = block * 128 + 128
        rows = slice(block * 128, hi)
        q_pos = lax.broadcasted_iota(jnp.int32, (128, hi - lo), 0) + block * 128
        k_pos = lax.broadcasted_iota(jnp.int32, (128, hi - lo), 1) + lo
        allowed = (meta_s[rows, 0:1] == seg_row[:, lo:hi]) & (k_pos <= q_pos)
        for g in range(2):
            cols = slice(g * HD, (g + 1) * HD)
            parts = []
            for j in range(2):
                one = q_s[j, rows, cols]
                parts.append(
                    (one * rope_c[rows, :] + pltpu.roll(one, HD // 2, 1) * rope_s[rows, :]).astype(BF)
                )
            scores = matmul_t(jnp.concatenate(parts, axis=0), k_s[lo:hi, cols])
            powers, totals = [], []
            for j in range(2):
                masked = jnp.where(allowed, scores[j * 128 : (j + 1) * 128], -1e30)
                largest = jnp.max(masked, axis=-1, keepdims=True)
                exponent = jnp.exp2((masked - largest) * SOFTMAX_SCALE)
                totals.append(jnp.sum(exponent, axis=-1, keepdims=True))
                powers.append(exponent.astype(BF))
            context = matmul(jnp.concatenate(powers, axis=0), v_s[lo:hi, cols])
            for j in range(2):
                weight = gate_s[rows, j : j + 1] / totals[j]
                ctx_s[j, rows, cols] = context[j * 128 : (j + 1) * 128] * weight
    for i, place in enumerate(head_order(True)):
        base = pl.multiple_of(place * ROWS, ROWS)
        take = pl.ds(base, ROWS)
        first = ctx_s[0, take, :].astype(BF)
        second = ctx_s[1, take, :].astype(BF)
        one = jnp.broadcast_to(meta_s[take, 1:2], (ROWS, 256)).astype(BF)
        two = jnp.broadcast_to(meta_s[take, 2:3], (ROWS, 256)).astype(BF)
        zero = jnp.zeros((ROWS, 256), BF)
        for e in range(8):
            number = jnp.full((ROWS, 256), e, BF)
            mix_s[i * ROWS : (i + 1) * ROWS, e * 256 : (e + 1) * 256] = jnp.where(
                one == number, first, jnp.where(two == number, second, zero)
            )

    out_copy.wait()

    def out_step(part, carry):
        cols = pl.ds(pl.multiple_of(part * 512, 512), 512)
        out = matmul(mix_s[...], wo_s[:, :, cols].reshape(8 * 256, 512))
        keep[:, cols] = out[:256].astype(BF)
        send[:, cols] = out[256:].astype(BF)
        return carry

    lax.fori_loop(0, 4, out_step, 0)


def attention(chunks, router, cos_t, sin_t, w_query, w_key, w_value, w_out):
    vmem = pl.BlockSpec(memory_space=pltpu.VMEM)
    hbm = pl.BlockSpec(memory_space=pltpu.MemorySpace.HBM)
    return pl.pallas_call(
        attention_body,
        in_specs=[vmem] * 11 + [hbm] * 4,
        out_specs=[vmem, vmem],
        scratch_shapes=[
            pltpu.VMEM((SEQ, D), BF),
            pltpu.VMEM((SEQ, META), F32),
            pltpu.VMEM((2, SEQ, HD), F32),
            pltpu.VMEM((2, SEQ, 256), F32),
            pltpu.VMEM((SEQ, 256), BF),
            pltpu.VMEM((SEQ, 256), BF),
            pltpu.VMEM((SEQ, HD), F32),
            pltpu.VMEM((SEQ, HD), F32),
            pltpu.VMEM((SEQ, META), F32),
            pltpu.VMEM((2, SEQ, 256), F32),
            pltpu.VMEM((SEQ, 8 * 256), BF),
            pltpu.VMEM((D, 8 * 256), BF),
            pltpu.VMEM((D, 512), BF),
            pltpu.VMEM((8, 256, D), BF),
            pltpu.SemaphoreType.DMA((11,)),
        ],
        out_shape=[
            jax.ShapeDtypeStruct((256, D), BF),
            jax.ShapeDtypeStruct((256, D), BF),
        ],
        compiler_params=pltpu.CompilerParams(vmem_limit_bytes=40 << 20),
        name="attention",
    )(*chunks, router, cos_t, sin_t, w_query, w_key, w_value, w_out)


def prepare_body(hidden, gain, segments, routes, out):
    out[:, :D] = normalize(hidden[...], gain[...])
    rows = jnp.concatenate([segments[...], routes[...], jnp.zeros((5, ROWS), jnp.int32)], axis=0).astype(F32)
    rows = jnp.concatenate([rows, jnp.zeros((META - 8, ROWS), F32)], axis=0)
    out[:, D:] = jnp.transpose(rows).astype(BF)


def prepare(hidden, gain, segments, routes):
    vmem = pl.BlockSpec(memory_space=pltpu.VMEM)
    return pl.pallas_call(
        prepare_body,
        in_specs=[vmem] * 4,
        out_specs=vmem,
        out_shape=jax.ShapeDtypeStruct((ROWS, D + META), BF),
        compiler_params=pltpu.CompilerParams(vmem_limit_bytes=8 << 20),
        name="prepare",
    )(hidden, gain, segments, routes)


def slot_rows(routes):
    first = routes[0:1, :]
    second = routes[1:2, :]
    expert = lax.broadcasted_iota(jnp.int32, (16, ROWS), 0)
    named = jnp.where((expert == first) | (expert == second), 1.0, 0.0)
    src = lax.broadcasted_iota(jnp.int32, (ROWS, ROWS), 0)
    dst = lax.broadcasted_iota(jnp.int32, (ROWS, ROWS), 1)
    rank = matmul(named.astype(BF), jnp.where(src < dst, 1.0, 0.0).astype(BF)).astype(jnp.int32)
    rank0 = jnp.sum(jnp.where(expert == first, rank, 0), axis=0, keepdims=True)
    rank1 = jnp.sum(jnp.where(expert == second, rank, 0), axis=0, keepdims=True)
    return first * SLOTS + rank0, second * SLOTS + rank1


def settle_body(hidden, keep, got, got_a, got_b, gain, routes, residual, rows):
    total = keep[:ROWS].astype(F32) + got[:ROWS].astype(F32) + got_a[:ROWS].astype(F32) + got_b[...].astype(F32)
    value = (hidden[...].astype(F32) + total).astype(BF)
    residual[...] = value
    normed = normalize(value, gain[...])
    slot0, slot1 = slot_rows(routes[...])
    row = lax.broadcasted_iota(jnp.int32, (8 * SLOTS, ROWS), 0)
    pick = jnp.where((row == slot0) | (row == slot1), 1.0, 0.0).astype(BF)
    rows[...] = matmul(pick, normed).astype(BF)


def settle(hidden, keep, got, got_a, got_b, gain, routes):
    vmem = pl.BlockSpec(memory_space=pltpu.VMEM)
    part = lambda n: pl.BlockSpec((n, D), lambda i: (0, 0))
    full = lambda shape: pl.BlockSpec(shape, lambda i: (0, 0))
    return pl.pallas_call(
        settle_body,
        grid=(1,),
        in_specs=[part(ROWS)] * 5 + [full((1, D)), full((2, ROWS))],
        out_specs=[part(ROWS), part(8 * SLOTS)],
        out_shape=[jax.ShapeDtypeStruct((ROWS, D), BF), jax.ShapeDtypeStruct((8 * SLOTS, D), BF)],
        compiler_params=pltpu.CompilerParams(vmem_limit_bytes=8 << 20),
        name="settle",
    )(hidden, keep, got, got_a, got_b, gain, routes)


def weigh_body(residual, gain, router, routes, high, low):
    normed = normalize(residual[...], gain[...])
    split = matmul_t(split_router(router[...]), normed)
    logits = split[0:8] + split[8:16] + split[16:24]
    expert = lax.broadcasted_iota(jnp.int32, (8, ROWS), 0)
    picked = routes[...]
    one = jnp.sum(jnp.where(expert == picked[0:1], logits, 0.0), axis=0, keepdims=True)
    two = jnp.sum(jnp.where(expert == picked[1:2], logits, 0.0), axis=0, keepdims=True)
    slot0, slot1 = slot_rows(picked)
    row = lax.broadcasted_iota(jnp.int32, (8 * SLOTS, ROWS), 0)
    table = jnp.where(row == slot0, 1.0 / (1.0 + jnp.exp(two - one)), 0.0) + jnp.where(
        row == slot1, 1.0 / (1.0 + jnp.exp(one - two)), 0.0
    )
    top = table.astype(BF)
    high[...] = top
    low[...] = (table - top.astype(F32)).astype(BF)


def weigh(residual, gain, router, routes):
    vmem = pl.BlockSpec(memory_space=pltpu.VMEM)
    return pl.pallas_call(
        weigh_body,
        in_specs=[vmem] * 4,
        out_specs=[vmem, vmem],
        out_shape=[jax.ShapeDtypeStruct((8 * SLOTS, ROWS), BF)] * 2,
        compiler_params=pltpu.CompilerParams(vmem_limit_bytes=8 << 20),
        name="weigh",
    )(residual, gain, router, routes)


def finish_body(residual, high, low, rows, out):
    values = rows[...]
    first_dim = (((0,), (0,)), ((), ()))
    mixture = lax.dot_general(high[...], values, first_dim, preferred_element_type=F32)
    mixture = mixture + lax.dot_general(low[...], values, first_dim, preferred_element_type=F32)
    out[...] = (residual[...].astype(F32) + mixture).astype(BF)


def finish(residual, high, low, rows):
    vmem = pl.BlockSpec(memory_space=pltpu.VMEM)
    return pl.pallas_call(
        finish_body,
        in_specs=[vmem] * 4,
        out_specs=vmem,
        out_shape=jax.ShapeDtypeStruct((ROWS, D), BF),
        compiler_params=pltpu.CompilerParams(vmem_limit_bytes=8 << 20),
        name="finish",
    )(residual, high, low, rows)


def pack_body(*refs):
    gus, gu_d, gu_e, downs = refs[:3], refs[3], refs[4], refs[5:9]
    out, sems = refs[9], refs[10]
    pieces = []
    for s in range(3):
        pieces.append((gus[s].at[0], s * HID, HID))
        pieces.append((gus[s].at[1], FF4 + s * HID, HID))
    pieces.append((gu_d.at[pl.ds(0, HID), :], 3 * HID, HID))
    pieces.append((gu_d.at[pl.ds(HID, CUT - HID), :], FF4 + 3 * HID, CUT - HID))
    pieces.append((gu_e, FF4 + 2 * HID + CUT, 2 * HID - CUT))
    for s in range(4):
        pieces.append((downs[s], 2 * FF4 + s * HID, HID))
    copies = [
        pltpu.make_async_copy(src, out.at[pl.ds(place, size), :], sems.at[i])
        for i, (src, place, size) in enumerate(pieces)
    ]
    for copy in copies:
        copy.start()
    for copy in copies:
        copy.wait()


def pack(gus, downs):
    return pl.pallas_call(
        pack_body,
        in_specs=[pl.BlockSpec(memory_space=pltpu.MemorySpace.HBM)] * 9,
        out_specs=pl.BlockSpec(memory_space=pltpu.VMEM),
        out_shape=pltpu.VMEM((3 * FF4, D), BF),
        scratch_shapes=[pltpu.SemaphoreType.DMA((13,))],
        compiler_params=pltpu.CompilerParams(vmem_limit_bytes=4 << 20),
        name="pack",
    )(*gus, *downs)


def expert_body(rows, weights, out, act_s):
    x = rows[...]
    for lo in range(0, FF4, 256):
        hi = min(lo + 256, FF4)
        gate = matmul_t(x, weights[lo:hi, :])
        up = matmul_t(x, weights[FF4 + lo : FF4 + hi, :])
        act_s[:, lo:hi] = (gate / (1.0 + jnp.exp(-gate)) * up).astype(BF)
    act = act_s[...]
    for lo in range(0, D, 256):
        out[:, lo : lo + 256] = matmul(act, weights[2 * FF4 :, lo : lo + 256]).astype(BF)


def experts(rows, weights):
    vmem = pl.BlockSpec(memory_space=pltpu.VMEM)
    return pl.pallas_call(
        expert_body,
        in_specs=[vmem] * 2,
        out_specs=vmem,
        out_shape=jax.ShapeDtypeStruct(rows.shape, BF),
        scratch_shapes=[pltpu.VMEM((rows.shape[0], FF4), BF)],
        compiler_params=pltpu.CompilerParams(vmem_limit_bytes=8 << 20),
    )(rows, weights)


def in_hbm(array):
    return pltpu.with_memory_space_constraint(array, pltpu.MemorySpace.HBM)


def per_device(
    hidden_in,
    segment_ids,
    attn_routes,
    ffn_routes,
    attn_gain,
    attn_router,
    w_query,
    w_key,
    w_value,
    w_out,
    ffn_gain,
    ffn_router,
    w_gate_up,
    w_down,
):
    gu = jnp.transpose(w_gate_up[0], (1, 2, 0))
    down = w_down[0]
    own = prepare(in_hbm(hidden_in), in_hbm(attn_gain[None, :]), in_hbm(segment_ids), in_hbm(attn_routes.T))
    chunks = gather_head(own)
    gu_x = send_xy(gu, WX)
    down_y = send_xy(down, WY)
    gu_y = send_xy(gu, WY)
    down_x = send_xy(down, WX)
    gu_xr = gu_x.reshape(2 * HID, D)[:CUT]
    gu_yr = gu_y.reshape(2 * HID, D)[CUT:]
    gu_d = send_xy(gu_xr, WY)
    gu_e = send_xy(gu_yr, WX)
    down_d = send_xy(down_y, WX)

    half = HD // 2
    inverse = ROPE_BASE ** (-jnp.arange(half, dtype=F32) / half)
    angles = jnp.arange(SEQ, dtype=F32)[:, None] * jnp.concatenate([inverse, inverse])[None, :]
    cosine, sine = jnp.cos(angles), jnp.sin(angles)
    keep, send = attention(
        chunks, in_hbm(attn_router.T), cosine, sine,
        in_hbm(w_query), in_hbm(w_key), in_hbm(w_value), in_hbm(w_out),
    )
    got = send_h(send, HC)
    pass_a = (keep[128:].astype(F32) + got[128:].astype(F32)).astype(BF)
    got_a = send_h(pass_a, HA)
    held = keep[64:128].astype(F32) + got[64:128].astype(F32) + got_a[64:].astype(F32)
    got_b = send_h(held.astype(BF), HB)
    residual, rows = settle(hidden_in, keep, got, got_a, got_b, ffn_gain[None, :], ffn_routes.T)
    arrived = lax.all_to_all(rows.reshape(8, SLOTS, D), "head", split_axis=0, concat_axis=0, tiled=True)
    high, low = weigh(residual, ffn_gain[None, :], ffn_router.T, ffn_routes.T)
    x_own = arrived.reshape(8 * SLOTS, D)
    weights = pack((in_hbm(gu), in_hbm(gu_x), in_hbm(gu_y), gu_d, gu_e), (in_hbm(down), down_x, down_y, down_d))
    x_d = send_xy(x_own, TXY)
    x_x = send_xy(x_own, TX)
    x_y = send_xy(x_own, TY)
    part = experts(x_own, weights)
    part_d = experts(x_d, weights)
    got_d = send_xy(part_d, TXY)
    part_x = experts(x_x, weights)
    got_x = send_xy(part_x, TX)
    part_y = experts(x_y, weights)
    got_y = send_xy(part_y, TY)
    rows = part.astype(F32) + got_d.astype(F32) + got_x.astype(F32) + got_y.astype(F32)
    rows = rows.astype(BF).reshape(8, SLOTS, D)
    returned = lax.all_to_all(rows, "head", split_axis=0, concat_axis=0, tiled=True)
    return finish(residual, high, low, returned.reshape(8 * SLOTS, D))


def solution(mesh):
    return jax.shard_map(
        per_device,
        mesh=mesh,
        in_specs=(
            P(("req", "head"), None),
            P("req", "head"),
            P(("req", "head"), None),
            P(("req", "head"), None),
            P(),
            P(),
            P(None, None, "head"),
            P(None, "head"),
            P(None, "head"),
            P(None, "head", None),
            P(),
            P(),
            P("head", None, None, "req"),
            P("head", "req", None),
        ),
        out_specs=P(("req", "head"), None),
        check_vma=False,
    )
```

```python
import functools
import math

import jax
import jax.numpy as jnp
from jax import lax
from jax.experimental import pallas as pl
from jax.experimental.pallas import tpu as pltpu
from jax.sharding import PartitionSpec as P


D = 2048
HD = 128
META = 128
ROWS = 64
SEQ = 512
SLOTS = 24
HID = 352
FF4 = 4 * HID
CUT = 3 * HID // 2
BF = jnp.bfloat16
F32 = jnp.float32
EPSILON = 1e-06
ROPE_BASE = 10000.0
SOFTMAX_SCALE = HD ** (-0.5) * math.log2(math.e)
AXES = ("req", "head")


def mate(v, parity):
    return v ^ 1 if parity == 0 else ((((v - 1) % 4) ^ 1) + 1) % 4


def square_perm(move_x, move_y, flip):
    pairs = []
    for i in range(128):
        r, h = divmod(i, 8)
        y, x = divmod(r, 4)
        parity = (h & 1) ^ flip
        ny = mate(y, parity ^ 1) if move_y else y
        nx = mate(x, parity) if move_x else x
        pairs.append((i, (ny * 4 + nx) * 8 + h))
    return pairs


WX, WY = square_perm(1, 0, 0), square_perm(0, 1, 0)
TX, TY, TXY = square_perm(1, 0, 1), square_perm(0, 1, 1), square_perm(1, 1, 1)
HA = [(h, h ^ (6 if h & 1 else 2)) for h in range(8)]
HB = [(h, h ^ (2 if h & 1 else 6)) for h in range(8)]
HC = [(h, h ^ 1) for h in range(8)]


def send_xy(v, pairs):
    return lax.ppermute(v, AXES, pairs)


def send_h(v, pairs):
    return lax.ppermute(v, "head", pairs)


def gather_head(own):
    a1 = send_h(own, HA)
    b1 = send_h(own, HB)
    c0 = send_h(own, HC)
    b2 = send_h(a1, HB)
    c1 = send_h(a1, HC)
    c2 = send_h(b1, HC)
    c3 = send_h(b2, HC)
    return [own, a1, b1, b2, c0, c1, c2, c3]


def head_order(scatter):
    h = lax.axis_index("head")
    m_a = 2 + 4 * (h & 1)
    m_b = 8 - m_a
    if scatter:
        m_a, m_b = m_b, m_a
        masks = (0, m_a, m_b, 4, 1, m_b ^ 1, m_a ^ 1, 5)
    else:
        masks = (0, m_a, m_b, 4, 1, m_b ^ 1, m_a ^ 1, 5)
    return [h ^ m for m in masks]


def split_router(router):
    hi = router.astype(BF).astype(F32)
    mid = (router - hi).astype(BF).astype(F32)
    low = router - hi - mid
    return jnp.concatenate([hi, mid, low, jnp.zeros_like(low)], axis=0).astype(BF)


def normalize(chunk, gain):
    wide = chunk.astype(F32)
    inverse = lax.rsqrt(jnp.mean(wide * wide, axis=-1, keepdims=True) + EPSILON)
    return (wide * inverse * gain).astype(BF)


def picked_gates(logits3, first, second):
    lane = lax.broadcasted_iota(jnp.int32, logits3.shape, 1)
    expert = (lane & 7).astype(F32)
    diff = jnp.where(expert == first, logits3, 0.0) - jnp.where(expert == second, logits3, 0.0)
    delta = jnp.sum(diff, axis=1, keepdims=True)
    return 1.0 / (1.0 + jnp.exp(-delta)), 1.0 / (1.0 + jnp.exp(delta))


def matmul(a, b):
    return jnp.dot(a, b, preferred_element_type=F32)


def matmul_t(a, b):
    return lax.dot_general(a, b, (((1,), (1,)), ((), ())), preferred_element_type=F32)


def attention_body(
    c0, c1, c2, c3, c4, c5, c6, c7,
    router, cos_t, sin_t, wq, wk, wv, wo,
    keep, send,
    x_s, meta_s, named_s, q_s, k_s, v_s, rope_c, rope_s, gate_s, ctx_s, mix_s, wq_s, kv_w, wo_s, sems,
):
    query_copies = [
        pltpu.make_async_copy(wq.at[e], wq_s.at[:, pl.ds(e * 256, 256)], sems.at[e]) for e in range(8)
    ]
    key_copy = pltpu.make_async_copy(wk, kv_w.at[:, pl.ds(0, 256)], sems.at[8])
    value_copy = pltpu.make_async_copy(wv, kv_w.at[:, pl.ds(256, 256)], sems.at[9])
    out_copy = pltpu.make_async_copy(wo, wo_s, sems.at[10])
    key_copy.start()
    value_copy.start()
    for copy in query_copies:
        copy.start()
    out_copy.start()

    for place, ref in zip(head_order(False), (c0, c1, c2, c3, c4, c5, c6, c7)):
        base = pl.multiple_of(place * ROWS, ROWS)
        x_s[pl.ds(base, ROWS), :] = ref[:, :D]
        meta_s[pl.ds(base, ROWS), :] = ref[:, D:].astype(F32)
    seg = meta_s[:, 0:1]
    for j in range(2):
        named_s[j] = jnp.broadcast_to(meta_s[:, 1 + j : 2 + j], (SEQ, HD))
    cos_all = cos_t[...]
    sin_all = sin_t[...]
    c_sel = jnp.broadcast_to(cos_t[0:1, :], (SEQ, HD))
    s_sel = jnp.broadcast_to(sin_t[0:1, :], (SEQ, HD))
    for number in (1, 2, 3):
        start = jnp.sum(jnp.where(seg < float(number), 1.0, 0.0)).astype(jnp.int32)
        start = jnp.minimum(start, SEQ - 1)
        here = seg == float(number)
        c_sel = jnp.where(here, cos_t[pl.ds(start, 1), :], c_sel)
        s_sel = jnp.where(here, sin_t[pl.ds(start, 1), :], s_sel)
    lane = lax.broadcasted_iota(jnp.int32, (SEQ, HD), 1)
    rope_c[...] = cos_all * c_sel + sin_all * s_sel
    turned = sin_all * c_sel - cos_all * s_sel
    rope_s[...] = jnp.where(lane < HD // 2, -turned, turned)
    logits3 = matmul_t(x_s[...], split_router(router[...]))
    g0, g1 = picked_gates(logits3, meta_s[:, 1:2], meta_s[:, 2:3])
    gate_s[:, 0:1] = g0
    gate_s[:, 1:2] = g1
    key_copy.wait()
    value_copy.wait()
    both = matmul(x_s[...], kv_w[...])
    v_s[...] = both[:, 256:].astype(BF)
    for g in range(2):
        one = both[:, g * HD : (g + 1) * HD]
        k_s[:, g * HD : (g + 1) * HD] = (
            one * rope_c[...] + pltpu.roll(one, HD // 2, 1) * rope_s[...]
        ).astype(BF)
    for copy in query_copies:
        copy.wait()

    def query_step(pair, carry):
        here = (2 * pair).astype(F32)
        query = matmul(x_s[...], wq_s[:, pl.ds(pl.multiple_of(pair * 512, 512), 512)])
        for j in range(2):
            is_first = named_s[j] == here
            is_second = named_s[j] == here + 1.0
            for g in range(2):
                cols = slice(g * HD, (g + 1) * HD)
                other = query[:, 256 + g * HD : 256 + (g + 1) * HD]
                q_s[j, :, cols] = jnp.where(
                    is_first, query[:, cols], jnp.where(is_second, other, q_s[j, :, cols])
                )
        return carry

    lax.fori_loop(0, 4, query_step, 0)
    seg_row = jnp.transpose(meta_s[...])[0:1, :]
    for block in range(4):
        lo = max(0, block * 128 - 256)
        hi = block * 128 + 128
        rows = slice(block * 128, hi)
        q_pos = lax.broadcasted_iota(jnp.int32, (128, hi - lo), 0) + block * 128
        k_pos = lax.broadcasted_iota(jnp.int32, (128, hi - lo), 1) + lo
        allowed = (meta_s[rows, 0:1] == seg_row[:, lo:hi]) & (k_pos <= q_pos)
        for g in range(2):
            cols = slice(g * HD, (g + 1) * HD)
            parts = []
            for j in range(2):
                one = q_s[j, rows, cols]
                parts.append(
                    (one * rope_c[rows, :] + pltpu.roll(one, HD // 2, 1) * rope_s[rows, :]).astype(BF)
                )
            scores = matmul_t(jnp.concatenate(parts, axis=0), k_s[lo:hi, cols])
            powers, totals = [], []
            for j in range(2):
                masked = jnp.where(allowed, scores[j * 128 : (j + 1) * 128], -1e30)
                largest = jnp.max(masked, axis=-1, keepdims=True)
                exponent = jnp.exp2((masked - largest) * SOFTMAX_SCALE)
                totals.append(jnp.sum(exponent, axis=-1, keepdims=True))
                powers.append(exponent.astype(BF))
            context = matmul(jnp.concatenate(powers, axis=0), v_s[lo:hi, cols])
            for j in range(2):
                weight = gate_s[rows, j : j + 1] / totals[j]
                ctx_s[j, rows, cols] = context[j * 128 : (j + 1) * 128] * weight
    for i, place in enumerate(head_order(True)):
        base = pl.multiple_of(place * ROWS, ROWS)
        take = pl.ds(base, ROWS)
        first = ctx_s[0, take, :].astype(BF)
        second = ctx_s[1, take, :].astype(BF)
        one = jnp.broadcast_to(meta_s[take, 1:2], (ROWS, 256)).astype(BF)
        two = jnp.broadcast_to(meta_s[take, 2:3], (ROWS, 256)).astype(BF)
        zero = jnp.zeros((ROWS, 256), BF)
        for e in range(8):
            number = jnp.full((ROWS, 256), e, BF)
            mix_s[i * ROWS : (i + 1) * ROWS, e * 256 : (e + 1) * 256] = jnp.where(
                one == number, first, jnp.where(two == number, second, zero)
            )

    out_copy.wait()

    def out_step(part, carry):
        cols = pl.ds(pl.multiple_of(part * 512, 512), 512)
        out = matmul(mix_s[...], wo_s[:, :, cols].reshape(8 * 256, 512))
        keep[:, cols] = out[:256].astype(BF)
        send[:, cols] = out[256:].astype(BF)
        return carry

    lax.fori_loop(0, 4, out_step, 0)


def attention(chunks, router, cos_t, sin_t, w_query, w_key, w_value, w_out):
    vmem = pl.BlockSpec(memory_space=pltpu.VMEM)
    hbm = pl.BlockSpec(memory_space=pltpu.MemorySpace.HBM)
    return pl.pallas_call(
        attention_body,
        in_specs=[vmem] * 11 + [hbm] * 4,
        out_specs=[vmem, vmem],
        scratch_shapes=[
            pltpu.VMEM((SEQ, D), BF),
            pltpu.VMEM((SEQ, META), F32),
            pltpu.VMEM((2, SEQ, HD), F32),
            pltpu.VMEM((2, SEQ, 256), F32),
            pltpu.VMEM((SEQ, 256), BF),
            pltpu.VMEM((SEQ, 256), BF),
            pltpu.VMEM((SEQ, HD), F32),
            pltpu.VMEM((SEQ, HD), F32),
            pltpu.VMEM((SEQ, META), F32),
            pltpu.VMEM((2, SEQ, 256), F32),
            pltpu.VMEM((SEQ, 8 * 256), BF),
            pltpu.VMEM((D, 8 * 256), BF),
            pltpu.VMEM((D, 512), BF),
            pltpu.VMEM((8, 256, D), BF),
            pltpu.SemaphoreType.DMA((11,)),
        ],
        out_shape=[
            jax.ShapeDtypeStruct((256, D), BF),
            jax.ShapeDtypeStruct((256, D), BF),
        ],
        compiler_params=pltpu.CompilerParams(vmem_limit_bytes=40 << 20),
        name="attention",
    )(*chunks, router, cos_t, sin_t, w_query, w_key, w_value, w_out)


def prepare_body(hidden, gain, segments, routes, out):
    out[:, :D] = normalize(hidden[...], gain[...])
    rows = jnp.concatenate([segments[...], routes[...], jnp.zeros((5, ROWS), jnp.int32)], axis=0).astype(F32)
    rows = jnp.concatenate([rows, jnp.zeros((META - 8, ROWS), F32)], axis=0)
    out[:, D:] = jnp.transpose(rows).astype(BF)


def prepare(hidden, gain, segments, routes):
    vmem = pl.BlockSpec(memory_space=pltpu.VMEM)
    return pl.pallas_call(
        prepare_body,
        in_specs=[vmem] * 4,
        out_specs=vmem,
        out_shape=jax.ShapeDtypeStruct((ROWS, D + META), BF),
        compiler_params=pltpu.CompilerParams(vmem_limit_bytes=8 << 20),
        name="prepare",
    )(hidden, gain, segments, routes)


def slot_rows(routes):
    first = routes[0:1, :]
    second = routes[1:2, :]
    expert = lax.broadcasted_iota(jnp.int32, (16, ROWS), 0)
    named = jnp.where((expert == first) | (expert == second), 1.0, 0.0)
    src = lax.broadcasted_iota(jnp.int32, (ROWS, ROWS), 0)
    dst = lax.broadcasted_iota(jnp.int32, (ROWS, ROWS), 1)
    rank = matmul(named.astype(BF), jnp.where(src < dst, 1.0, 0.0).astype(BF)).astype(jnp.int32)
    rank0 = jnp.sum(jnp.where(expert == first, rank, 0), axis=0, keepdims=True)
    rank1 = jnp.sum(jnp.where(expert == second, rank, 0), axis=0, keepdims=True)
    return first * SLOTS + rank0, second * SLOTS + rank1


def settle_body(hidden, keep, got, got_a, got_b, gain, routes, residual, rows):
    total = keep[:ROWS].astype(F32) + got[:ROWS].astype(F32) + got_a[:ROWS].astype(F32) + got_b[...].astype(F32)
    value = (hidden[...].astype(F32) + total).astype(BF)
    residual[...] = value
    normed = normalize(value, gain[...])
    slot0, slot1 = slot_rows(routes[...])
    row = lax.broadcasted_iota(jnp.int32, (8 * SLOTS, ROWS), 0)
    pick = jnp.where((row == slot0) | (row == slot1), 1.0, 0.0).astype(BF)
    rows[...] = matmul(pick, normed).astype(BF)


def settle(hidden, keep, got, got_a, got_b, gain, routes):
    vmem = pl.BlockSpec(memory_space=pltpu.VMEM)
    part = lambda n: pl.BlockSpec((n, D), lambda i: (0, 0))
    full = lambda shape: pl.BlockSpec(shape, lambda i: (0, 0))
    return pl.pallas_call(
        settle_body,
        grid=(1,),
        in_specs=[part(ROWS)] * 5 + [full((1, D)), full((2, ROWS))],
        out_specs=[part(ROWS), part(8 * SLOTS)],
        out_shape=[jax.ShapeDtypeStruct((ROWS, D), BF), jax.ShapeDtypeStruct((8 * SLOTS, D), BF)],
        compiler_params=pltpu.CompilerParams(vmem_limit_bytes=8 << 20),
        name="settle",
    )(hidden, keep, got, got_a, got_b, gain, routes)


def weigh_body(residual, gain, router, routes, high, low):
    normed = normalize(residual[...], gain[...])
    split = matmul_t(split_router(router[...]), normed)
    logits = split[0:8] + split[8:16] + split[16:24]
    expert = lax.broadcasted_iota(jnp.int32, (8, ROWS), 0)
    picked = routes[...]
    one = jnp.sum(jnp.where(expert == picked[0:1], logits, 0.0), axis=0, keepdims=True)
    two = jnp.sum(jnp.where(expert == picked[1:2], logits, 0.0), axis=0, keepdims=True)
    slot0, slot1 = slot_rows(picked)
    row = lax.broadcasted_iota(jnp.int32, (8 * SLOTS, ROWS), 0)
    table = jnp.where(row == slot0, 1.0 / (1.0 + jnp.exp(two - one)), 0.0) + jnp.where(
        row == slot1, 1.0 / (1.0 + jnp.exp(one - two)), 0.0
    )
    top = table.astype(BF)
    high[...] = top
    low[...] = (table - top.astype(F32)).astype(BF)


def weigh(residual, gain, router, routes):
    vmem = pl.BlockSpec(memory_space=pltpu.VMEM)
    return pl.pallas_call(
        weigh_body,
        in_specs=[vmem] * 4,
        out_specs=[vmem, vmem],
        out_shape=[jax.ShapeDtypeStruct((8 * SLOTS, ROWS), BF)] * 2,
        compiler_params=pltpu.CompilerParams(vmem_limit_bytes=8 << 20),
        name="weigh",
    )(residual, gain, router, routes)


def finish_body(residual, high, low, rows, out):
    values = rows[...]
    first_dim = (((0,), (0,)), ((), ()))
    mixture = lax.dot_general(high[...], values, first_dim, preferred_element_type=F32)
    mixture = mixture + lax.dot_general(low[...], values, first_dim, preferred_element_type=F32)
    out[...] = (residual[...].astype(F32) + mixture).astype(BF)


def finish(residual, high, low, rows):
    vmem = pl.BlockSpec(memory_space=pltpu.VMEM)
    return pl.pallas_call(
        finish_body,
        in_specs=[vmem] * 4,
        out_specs=vmem,
        out_shape=jax.ShapeDtypeStruct((ROWS, D), BF),
        compiler_params=pltpu.CompilerParams(vmem_limit_bytes=8 << 20),
        name="finish",
    )(residual, high, low, rows)


def pack_body(*refs):
    gus, gu_d, gu_e, downs = refs[:3], refs[3], refs[4], refs[5:9]
    out, sems = refs[9], refs[10]
    pieces = []
    for s in range(3):
        pieces.append((gus[s].at[0], s * HID, HID))
        pieces.append((gus[s].at[1], FF4 + s * HID, HID))
    pieces.append((gu_d.at[pl.ds(0, HID), :], 3 * HID, HID))
    pieces.append((gu_d.at[pl.ds(HID, CUT - HID), :], FF4 + 3 * HID, CUT - HID))
    pieces.append((gu_e, FF4 + 2 * HID + CUT, 2 * HID - CUT))
    for s in range(4):
        pieces.append((downs[s], 2 * FF4 + s * HID, HID))
    copies = [
        pltpu.make_async_copy(src, out.at[pl.ds(place, size), :], sems.at[i])
        for i, (src, place, size) in enumerate(pieces)
    ]
    for copy in copies:
        copy.start()
    for copy in copies:
        copy.wait()


def pack(gus, downs):
    return pl.pallas_call(
        pack_body,
        in_specs=[pl.BlockSpec(memory_space=pltpu.MemorySpace.HBM)] * 9,
        out_specs=pl.BlockSpec(memory_space=pltpu.VMEM),
        out_shape=pltpu.VMEM((3 * FF4, D), BF),
        scratch_shapes=[pltpu.SemaphoreType.DMA((13,))],
        compiler_params=pltpu.CompilerParams(vmem_limit_bytes=4 << 20),
        name="pack",
    )(*gus, *downs)


def expert_body(count, *refs):
    weights, outs = refs[count], refs[count + 1 : 2 * count + 1]
    act_s = refs[-1]
    if count == 1:
        x = refs[0][...]
    else:
        x = jnp.concatenate([ref[...] for ref in refs[:count]], axis=0)
    for lo in range(0, FF4, 256):
        hi = min(lo + 256, FF4)
        gate = matmul_t(x, weights[lo:hi, :])
        up = matmul_t(x, weights[FF4 + lo : FF4 + hi, :])
        act_s[:, lo:hi] = (gate / (1.0 + jnp.exp(-gate)) * up).astype(BF)
    act = act_s[...]
    size = 8 * SLOTS
    for lo in range(0, D, 256):
        result = matmul(act, weights[2 * FF4 :, lo : lo + 256]).astype(BF)
        for i, out in enumerate(outs):
            out[:, lo : lo + 256] = result[i * size : (i + 1) * size]


def experts(blocks, weights):
    vmem = pl.BlockSpec(memory_space=pltpu.VMEM)
    count = len(blocks)
    return pl.pallas_call(
        functools.partial(expert_body, count),
        in_specs=[vmem] * (count + 1),
        out_specs=[vmem] * count,
        out_shape=[jax.ShapeDtypeStruct((8 * SLOTS, D), BF)] * count,
        scratch_shapes=[pltpu.VMEM((count * 8 * SLOTS, FF4), BF)],
        compiler_params=pltpu.CompilerParams(vmem_limit_bytes=12 << 20),
    )(*blocks, weights)


def in_hbm(array):
    return pltpu.with_memory_space_constraint(array, pltpu.MemorySpace.HBM)


def per_device(
    hidden_in,
    segment_ids,
    attn_routes,
    ffn_routes,
    attn_gain,
    attn_router,
    w_query,
    w_key,
    w_value,
    w_out,
    ffn_gain,
    ffn_router,
    w_gate_up,
    w_down,
):
    gu = jnp.transpose(w_gate_up[0], (1, 2, 0))
    down = w_down[0]
    own = prepare(in_hbm(hidden_in), in_hbm(attn_gain[None, :]), in_hbm(segment_ids), in_hbm(attn_routes.T))
    chunks = gather_head(own)
    gu_x = send_xy(gu, WX)
    down_y = send_xy(down, WY)
    gu_y = send_xy(gu, WY)
    down_x = send_xy(down, WX)
    gu_xr = gu_x.reshape(2 * HID, D)[:CUT]
    gu_yr = gu_y.reshape(2 * HID, D)[CUT:]
    gu_d = send_xy(gu_xr, WY)
    gu_e = send_xy(gu_yr, WX)
    down_d = send_xy(down_y, WX)

    half = HD // 2
    inverse = ROPE_BASE ** (-jnp.arange(half, dtype=F32) / half)
    angles = jnp.arange(SEQ, dtype=F32)[:, None] * jnp.concatenate([inverse, inverse])[None, :]
    cosine, sine = jnp.cos(angles), jnp.sin(angles)
    keep, send = attention(
        chunks, in_hbm(attn_router.T), cosine, sine,
        in_hbm(w_query), in_hbm(w_key), in_hbm(w_value), in_hbm(w_out),
    )
    got = send_h(send, HC)
    pass_a = (keep[128:].astype(F32) + got[128:].astype(F32)).astype(BF)
    got_a = send_h(pass_a, HA)
    held = keep[64:128].astype(F32) + got[64:128].astype(F32) + got_a[64:].astype(F32)
    got_b = send_h(held.astype(BF), HB)
    residual, rows = settle(hidden_in, keep, got, got_a, got_b, ffn_gain[None, :], ffn_routes.T)
    arrived = lax.all_to_all(rows.reshape(8, SLOTS, D), "head", split_axis=0, concat_axis=0, tiled=True)
    high, low = weigh(residual, ffn_gain[None, :], ffn_router.T, ffn_routes.T)
    x_own = arrived.reshape(8 * SLOTS, D)
    weights = pack((in_hbm(gu), in_hbm(gu_x), in_hbm(gu_y), gu_d, gu_e), (in_hbm(down), down_x, down_y, down_d))
    x_d = send_xy(x_own, TXY)
    x_x = send_xy(x_own, TX)
    x_y = send_xy(x_own, TY)
    (part_d,) = experts([x_d], weights)
    got_d = send_xy(part_d, TXY)
    part_x, part_y = experts([x_x, x_y], weights)
    got_x = send_xy(part_x, TX)
    got_y = send_xy(part_y, TY)
    (part,) = experts([x_own], weights)
    rows = part.astype(F32) + got_d.astype(F32) + got_x.astype(F32) + got_y.astype(F32)
    rows = rows.astype(BF).reshape(8, SLOTS, D)
    returned = lax.all_to_all(rows, "head", split_axis=0, concat_axis=0, tiled=True)
    return finish(residual, high, low, returned.reshape(8 * SLOTS, D))


def solution(mesh):
    return jax.shard_map(
        per_device,
        mesh=mesh,
        in_specs=(
            P(("req", "head"), None),
            P("req", "head"),
            P(("req", "head"), None),
            P(("req", "head"), None),
            P(),
            P(),
            P(None, None, "head"),
            P(None, "head"),
            P(None, "head"),
            P(None, "head", None),
            P(),
            P(),
            P("head", None, None, "req"),
            P("head", "req", None),
        ),
        out_specs=P(("req", "head"), None),
        check_vma=False,
    )
```

```python
import functools
import math

import jax
import jax.numpy as jnp
from jax import lax
from jax.experimental import pallas as pl
from jax.experimental.pallas import tpu as pltpu
from jax.sharding import PartitionSpec as P


D = 2048
HD = 128
META = 128
ROWS = 64
SEQ = 512
SLOTS = 24
HID = 352
FF4 = 4 * HID
CUT = 3 * HID // 2
BF = jnp.bfloat16
F32 = jnp.float32
EPSILON = 1e-06
ROPE_BASE = 10000.0
SOFTMAX_SCALE = HD ** (-0.5) * math.log2(math.e)
AXES = ("req", "head")


def mate(v, parity):
    return v ^ 1 if parity == 0 else ((((v - 1) % 4) ^ 1) + 1) % 4


def square_perm(move_x, move_y, flip):
    pairs = []
    for i in range(128):
        r, h = divmod(i, 8)
        y, x = divmod(r, 4)
        parity = (h & 1) ^ flip
        ny = mate(y, parity ^ 1) if move_y else y
        nx = mate(x, parity) if move_x else x
        pairs.append((i, (ny * 4 + nx) * 8 + h))
    return pairs


WX, WY = square_perm(1, 0, 0), square_perm(0, 1, 0)
TX, TY, TXY = square_perm(1, 0, 1), square_perm(0, 1, 1), square_perm(1, 1, 1)
HA = [(h, h ^ (6 if h & 1 else 2)) for h in range(8)]
HB = [(h, h ^ (2 if h & 1 else 6)) for h in range(8)]
HC = [(h, h ^ 1) for h in range(8)]


def send_xy(v, pairs):
    return lax.ppermute(v, AXES, pairs)


def send_h(v, pairs):
    return lax.ppermute(v, "head", pairs)


def gather_head(own):
    a1 = send_h(own, HA)
    b1 = send_h(own, HB)
    c0 = send_h(own, HC)
    b2 = send_h(a1, HB)
    c1 = send_h(a1, HC)
    c2 = send_h(b1, HC)
    c3 = send_h(b2, HC)
    return [own, a1, b1, b2, c0, c1, c2, c3]


def head_order(scatter):
    h = lax.axis_index("head")
    m_a = 2 + 4 * (h & 1)
    m_b = 8 - m_a
    if scatter:
        m_a, m_b = m_b, m_a
        masks = (0, m_a, m_b, 4, 1, m_b ^ 1, m_a ^ 1, 5)
    else:
        masks = (0, m_a, m_b, 4, 1, m_b ^ 1, m_a ^ 1, 5)
    return [h ^ m for m in masks]


def split_router(router):
    hi = router.astype(BF).astype(F32)
    mid = (router - hi).astype(BF).astype(F32)
    low = router - hi - mid
    return jnp.concatenate([hi, mid, low, jnp.zeros_like(low)], axis=0).astype(BF)


def normalize(chunk, gain):
    wide = chunk.astype(F32)
    inverse = lax.rsqrt(jnp.mean(wide * wide, axis=-1, keepdims=True) + EPSILON)
    return (wide * inverse * gain).astype(BF)


def picked_gates(logits3, first, second):
    lane = lax.broadcasted_iota(jnp.int32, logits3.shape, 1)
    expert = (lane & 7).astype(F32)
    diff = jnp.where(expert == first, logits3, 0.0) - jnp.where(expert == second, logits3, 0.0)
    delta = jnp.sum(diff, axis=1, keepdims=True)
    return 1.0 / (1.0 + jnp.exp(-delta)), 1.0 / (1.0 + jnp.exp(delta))


def matmul(a, b):
    return jnp.dot(a, b, preferred_element_type=F32)


def matmul_t(a, b):
    return lax.dot_general(a, b, (((1,), (1,)), ((), ())), preferred_element_type=F32)


def attention_body(
    c0, c1, c2, c3, c4, c5, c6, c7,
    router, cos_t, sin_t, wq, wk, wv, wo,
    keep, send,
    x_s, meta_s, named_s, q_s, k_s, v_s, rope_c, rope_s, gate_s, ctx_s, mix_s, wq_s, kv_w, wo_s, sems,
):
    query_copies = [
        pltpu.make_async_copy(wq.at[e], wq_s.at[:, pl.ds(e * 256, 256)], sems.at[e]) for e in range(8)
    ]
    key_copy = pltpu.make_async_copy(wk, kv_w.at[:, pl.ds(0, 256)], sems.at[8])
    value_copy = pltpu.make_async_copy(wv, kv_w.at[:, pl.ds(256, 256)], sems.at[9])
    out_copy = pltpu.make_async_copy(wo, wo_s, sems.at[10])
    key_copy.start()
    value_copy.start()
    for copy in query_copies:
        copy.start()
    out_copy.start()

    for place, ref in zip(head_order(False), (c0, c1, c2, c3, c4, c5, c6, c7)):
        base = pl.multiple_of(place * ROWS, ROWS)
        x_s[pl.ds(base, ROWS), :] = ref[:, :D]
        meta_s[pl.ds(base, ROWS), :] = ref[:, D:].astype(F32)
    seg = meta_s[:, 0:1]
    for j in range(2):
        named_s[j] = jnp.broadcast_to(meta_s[:, 1 + j : 2 + j], (SEQ, HD))
    cos_all = cos_t[...]
    sin_all = sin_t[...]
    c_sel = jnp.broadcast_to(cos_t[0:1, :], (SEQ, HD))
    s_sel = jnp.broadcast_to(sin_t[0:1, :], (SEQ, HD))
    for number in (1, 2, 3):
        start = jnp.sum(jnp.where(seg < float(number), 1.0, 0.0)).astype(jnp.int32)
        start = jnp.minimum(start, SEQ - 1)
        here = seg == float(number)
        c_sel = jnp.where(here, cos_t[pl.ds(start, 1), :], c_sel)
        s_sel = jnp.where(here, sin_t[pl.ds(start, 1), :], s_sel)
    lane = lax.broadcasted_iota(jnp.int32, (SEQ, HD), 1)
    rope_c[...] = cos_all * c_sel + sin_all * s_sel
    turned = sin_all * c_sel - cos_all * s_sel
    rope_s[...] = jnp.where(lane < HD // 2, -turned, turned)
    logits3 = matmul_t(x_s[...], split_router(router[...]))
    g0, g1 = picked_gates(logits3, meta_s[:, 1:2], meta_s[:, 2:3])
    gate_s[:, 0:1] = g0
    gate_s[:, 1:2] = g1
    key_copy.wait()
    value_copy.wait()
    both = matmul(x_s[...], kv_w[...])
    v_s[...] = both[:, 256:].astype(BF)
    for g in range(2):
        one = both[:, g * HD : (g + 1) * HD]
        k_s[:, g * HD : (g + 1) * HD] = (
            one * rope_c[...] + pltpu.roll(one, HD // 2, 1) * rope_s[...]
        ).astype(BF)

    def query_step(pair, carry):
        for side in range(2):
            e = 2 * pair + side
            place = pl.ds(pl.multiple_of(e * 256, 256), 256)
            pltpu.make_async_copy(wq.at[e], wq_s.at[:, place], sems.at[e]).wait()
        here = (2 * pair).astype(F32)
        query = matmul(x_s[...], wq_s[:, pl.ds(pl.multiple_of(pair * 512, 512), 512)])
        for j in range(2):
            is_first = named_s[j] == here
            is_second = named_s[j] == here + 1.0
            for g in range(2):
                cols = slice(g * HD, (g + 1) * HD)
                other = query[:, 256 + g * HD : 256 + (g + 1) * HD]
                q_s[j, :, cols] = jnp.where(
                    is_first, query[:, cols], jnp.where(is_second, other, q_s[j, :, cols])
                )
        return carry

    lax.fori_loop(0, 4, query_step, 0)
    seg_row = jnp.transpose(meta_s[...])[0:1, :]
    for block in range(4):
        lo = max(0, block * 128 - 256)
        hi = block * 128 + 128
        rows = slice(block * 128, hi)
        q_pos = lax.broadcasted_iota(jnp.int32, (128, hi - lo), 0) + block * 128
        k_pos = lax.broadcasted_iota(jnp.int32, (128, hi - lo), 1) + lo
        allowed = (meta_s[rows, 0:1] == seg_row[:, lo:hi]) & (k_pos <= q_pos)
        for g in range(2):
            cols = slice(g * HD, (g + 1) * HD)
            parts = []
            for j in range(2):
                one = q_s[j, rows, cols]
                parts.append(
                    (one * rope_c[rows, :] + pltpu.roll(one, HD // 2, 1) * rope_s[rows, :]).astype(BF)
                )
            scores = matmul_t(jnp.concatenate(parts, axis=0), k_s[lo:hi, cols])
            powers, totals = [], []
            for j in range(2):
                masked = jnp.where(allowed, scores[j * 128 : (j + 1) * 128], -1e30)
                largest = jnp.max(masked, axis=-1, keepdims=True)
                exponent = jnp.exp2((masked - largest) * SOFTMAX_SCALE)
                totals.append(jnp.sum(exponent, axis=-1, keepdims=True))
                powers.append(exponent.astype(BF))
            context = matmul(jnp.concatenate(powers, axis=0), v_s[lo:hi, cols])
            for j in range(2):
                weight = gate_s[rows, j : j + 1] / totals[j]
                ctx_s[j, rows, cols] = context[j * 128 : (j + 1) * 128] * weight
    for i, place in enumerate(head_order(True)):
        base = pl.multiple_of(place * ROWS, ROWS)
        take = pl.ds(base, ROWS)
        first = ctx_s[0, take, :].astype(BF)
        second = ctx_s[1, take, :].astype(BF)
        one = jnp.broadcast_to(meta_s[take, 1:2], (ROWS, 256)).astype(BF)
        two = jnp.broadcast_to(meta_s[take, 2:3], (ROWS, 256)).astype(BF)
        zero = jnp.zeros((ROWS, 256), BF)
        for e in range(8):
            number = jnp.full((ROWS, 256), e, BF)
            mix_s[i * ROWS : (i + 1) * ROWS, e * 256 : (e + 1) * 256] = jnp.where(
                one == number, first, jnp.where(two == number, second, zero)
            )

    out_copy.wait()

    def out_step(part, carry):
        cols = pl.ds(pl.multiple_of(part * 512, 512), 512)
        out = matmul(mix_s[...], wo_s[:, :, cols].reshape(8 * 256, 512))
        keep[:, cols] = out[:256].astype(BF)
        send[:, cols] = out[256:].astype(BF)
        return carry

    lax.fori_loop(0, 4, out_step, 0)


def attention(chunks, router, cos_t, sin_t, w_query, w_key, w_value, w_out):
    vmem = pl.BlockSpec(memory_space=pltpu.VMEM)
    hbm = pl.BlockSpec(memory_space=pltpu.MemorySpace.HBM)
    return pl.pallas_call(
        attention_body,
        in_specs=[vmem] * 11 + [hbm] * 4,
        out_specs=[vmem, vmem],
        scratch_shapes=[
            pltpu.VMEM((SEQ, D), BF),
            pltpu.VMEM((SEQ, META), F32),
            pltpu.VMEM((2, SEQ, HD), F32),
            pltpu.VMEM((2, SEQ, 256), F32),
            pltpu.VMEM((SEQ, 256), BF),
            pltpu.VMEM((SEQ, 256), BF),
            pltpu.VMEM((SEQ, HD), F32),
            pltpu.VMEM((SEQ, HD), F32),
            pltpu.VMEM((SEQ, META), F32),
            pltpu.VMEM((2, SEQ, 256), F32),
            pltpu.VMEM((SEQ, 8 * 256), BF),
            pltpu.VMEM((D, 8 * 256), BF),
            pltpu.VMEM((D, 512), BF),
            pltpu.VMEM((8, 256, D), BF),
            pltpu.SemaphoreType.DMA((11,)),
        ],
        out_shape=[
            jax.ShapeDtypeStruct((256, D), BF),
            jax.ShapeDtypeStruct((256, D), BF),
        ],
        compiler_params=pltpu.CompilerParams(vmem_limit_bytes=40 << 20),
        name="attention",
    )(*chunks, router, cos_t, sin_t, w_query, w_key, w_value, w_out)


def prepare_body(hidden, gain, segments, routes, out):
    out[:, :D] = normalize(hidden[...], gain[...])
    rows = jnp.concatenate([segments[...], routes[...], jnp.zeros((5, ROWS), jnp.int32)], axis=0).astype(F32)
    rows = jnp.concatenate([rows, jnp.zeros((META - 8, ROWS), F32)], axis=0)
    out[:, D:] = jnp.transpose(rows).astype(BF)


def prepare(hidden, gain, segments, routes):
    vmem = pl.BlockSpec(memory_space=pltpu.VMEM)
    return pl.pallas_call(
        prepare_body,
        in_specs=[vmem] * 4,
        out_specs=vmem,
        out_shape=jax.ShapeDtypeStruct((ROWS, D + META), BF),
        compiler_params=pltpu.CompilerParams(vmem_limit_bytes=8 << 20),
        name="prepare",
    )(hidden, gain, segments, routes)


def slot_rows(routes):
    first = routes[0:1, :]
    second = routes[1:2, :]
    expert = lax.broadcasted_iota(jnp.int32, (16, ROWS), 0)
    named = jnp.where((expert == first) | (expert == second), 1.0, 0.0)
    src = lax.broadcasted_iota(jnp.int32, (ROWS, ROWS), 0)
    dst = lax.broadcasted_iota(jnp.int32, (ROWS, ROWS), 1)
    rank = matmul(named.astype(BF), jnp.where(src < dst, 1.0, 0.0).astype(BF)).astype(jnp.int32)
    rank0 = jnp.sum(jnp.where(expert == first, rank, 0), axis=0, keepdims=True)
    rank1 = jnp.sum(jnp.where(expert == second, rank, 0), axis=0, keepdims=True)
    return first * SLOTS + rank0, second * SLOTS + rank1


def settle_body(hidden, keep, got, got_a, got_b, gain, routes, residual, rows):
    total = keep[:ROWS].astype(F32) + got[:ROWS].astype(F32) + got_a[:ROWS].astype(F32) + got_b[...].astype(F32)
    value = (hidden[...].astype(F32) + total).astype(BF)
    residual[...] = value
    normed = normalize(value, gain[...])
    slot0, slot1 = slot_rows(routes[...])
    row = lax.broadcasted_iota(jnp.int32, (8 * SLOTS, ROWS), 0)
    pick = jnp.where((row == slot0) | (row == slot1), 1.0, 0.0).astype(BF)
    rows[...] = matmul(pick, normed).astype(BF)


def settle(hidden, keep, got, got_a, got_b, gain, routes):
    vmem = pl.BlockSpec(memory_space=pltpu.VMEM)
    part = lambda n: pl.BlockSpec((n, D), lambda i: (0, 0))
    full = lambda shape: pl.BlockSpec(shape, lambda i: (0, 0))
    return pl.pallas_call(
        settle_body,
        grid=(1,),
        in_specs=[part(ROWS)] * 5 + [full((1, D)), full((2, ROWS))],
        out_specs=[part(ROWS), part(8 * SLOTS)],
        out_shape=[jax.ShapeDtypeStruct((ROWS, D), BF), jax.ShapeDtypeStruct((8 * SLOTS, D), BF)],
        compiler_params=pltpu.CompilerParams(vmem_limit_bytes=8 << 20),
        name="settle",
    )(hidden, keep, got, got_a, got_b, gain, routes)


def weigh_body(residual, gain, router, routes, high, low):
    normed = normalize(residual[...], gain[...])
    split = matmul_t(split_router(router[...]), normed)
    logits = split[0:8] + split[8:16] + split[16:24]
    expert = lax.broadcasted_iota(jnp.int32, (8, ROWS), 0)
    picked = routes[...]
    one = jnp.sum(jnp.where(expert == picked[0:1], logits, 0.0), axis=0, keepdims=True)
    two = jnp.sum(jnp.where(expert == picked[1:2], logits, 0.0), axis=0, keepdims=True)
    slot0, slot1 = slot_rows(picked)
    row = lax.broadcasted_iota(jnp.int32, (8 * SLOTS, ROWS), 0)
    table = jnp.where(row == slot0, 1.0 / (1.0 + jnp.exp(two - one)), 0.0) + jnp.where(
        row == slot1, 1.0 / (1.0 + jnp.exp(one - two)), 0.0
    )
    top = table.astype(BF)
    high[...] = top
    low[...] = (table - top.astype(F32)).astype(BF)


def weigh(residual, gain, router, routes):
    vmem = pl.BlockSpec(memory_space=pltpu.VMEM)
    return pl.pallas_call(
        weigh_body,
        in_specs=[vmem] * 4,
        out_specs=[vmem, vmem],
        out_shape=[jax.ShapeDtypeStruct((8 * SLOTS, ROWS), BF)] * 2,
        compiler_params=pltpu.CompilerParams(vmem_limit_bytes=8 << 20),
        name="weigh",
    )(residual, gain, router, routes)


def finish_body(residual, high, low, rows, out):
    values = rows[...]
    first_dim = (((0,), (0,)), ((), ()))
    mixture = lax.dot_general(high[...], values, first_dim, preferred_element_type=F32)
    mixture = mixture + lax.dot_general(low[...], values, first_dim, preferred_element_type=F32)
    out[...] = (residual[...].astype(F32) + mixture).astype(BF)


def finish(residual, high, low, rows):
    vmem = pl.BlockSpec(memory_space=pltpu.VMEM)
    return pl.pallas_call(
        finish_body,
        in_specs=[vmem] * 4,
        out_specs=vmem,
        out_shape=jax.ShapeDtypeStruct((ROWS, D), BF),
        compiler_params=pltpu.CompilerParams(vmem_limit_bytes=8 << 20),
        name="finish",
    )(residual, high, low, rows)


def pack_body(*refs):
    gus, gu_d, gu_e, downs = refs[:3], refs[3], refs[4], refs[5:9]
    out, sems = refs[9], refs[10]
    pieces = []
    for s in range(3):
        pieces.append((gus[s].at[0], s * HID, HID))
        pieces.append((gus[s].at[1], FF4 + s * HID, HID))
    pieces.append((gu_d.at[pl.ds(0, HID), :], 3 * HID, HID))
    pieces.append((gu_d.at[pl.ds(HID, CUT - HID), :], FF4 + 3 * HID, CUT - HID))
    pieces.append((gu_e, FF4 + 2 * HID + CUT, 2 * HID - CUT))
    for s in range(4):
        pieces.append((downs[s], 2 * FF4 + s * HID, HID))
    copies = [
        pltpu.make_async_copy(src, out.at[pl.ds(place, size), :], sems.at[i])
        for i, (src, place, size) in enumerate(pieces)
    ]
    for copy in copies:
        copy.start()
    for copy in copies:
        copy.wait()


def pack(gus, downs):
    return pl.pallas_call(
        pack_body,
        in_specs=[pl.BlockSpec(memory_space=pltpu.MemorySpace.HBM)] * 9,
        out_specs=pl.BlockSpec(memory_space=pltpu.VMEM),
        out_shape=pltpu.VMEM((3 * FF4, D), BF),
        scratch_shapes=[pltpu.SemaphoreType.DMA((13,))],
        compiler_params=pltpu.CompilerParams(vmem_limit_bytes=4 << 20),
        name="pack",
    )(*gus, *downs)


def expert_body(count, *refs):
    weights, outs = refs[count], refs[count + 1 : 2 * count + 1]
    act_s = refs[-1]
    if count == 1:
        x = refs[0][...]
    else:
        x = jnp.concatenate([ref[...] for ref in refs[:count]], axis=0)
    for lo in range(0, FF4, 256):
        hi = min(lo + 256, FF4)
        gate = matmul_t(x, weights[lo:hi, :])
        up = matmul_t(x, weights[FF4 + lo : FF4 + hi, :])
        act_s[:, lo:hi] = (gate / (1.0 + jnp.exp(-gate)) * up).astype(BF)
    act = act_s[...]
    size = 8 * SLOTS
    for lo in range(0, D, 256):
        result = matmul(act, weights[2 * FF4 :, lo : lo + 256]).astype(BF)
        for i, out in enumerate(outs):
            out[:, lo : lo + 256] = result[i * size : (i + 1) * size]


def experts(blocks, weights):
    vmem = pl.BlockSpec(memory_space=pltpu.VMEM)
    count = len(blocks)
    return pl.pallas_call(
        functools.partial(expert_body, count),
        in_specs=[vmem] * (count + 1),
        out_specs=[vmem] * count,
        out_shape=[jax.ShapeDtypeStruct((8 * SLOTS, D), BF)] * count,
        scratch_shapes=[pltpu.VMEM((count * 8 * SLOTS, FF4), BF)],
        compiler_params=pltpu.CompilerParams(vmem_limit_bytes=12 << 20),
    )(*blocks, weights)


def in_hbm(array):
    return pltpu.with_memory_space_constraint(array, pltpu.MemorySpace.HBM)


def per_device(
    hidden_in,
    segment_ids,
    attn_routes,
    ffn_routes,
    attn_gain,
    attn_router,
    w_query,
    w_key,
    w_value,
    w_out,
    ffn_gain,
    ffn_router,
    w_gate_up,
    w_down,
):
    gu = jnp.transpose(w_gate_up[0], (1, 2, 0))
    down = w_down[0]
    own = prepare(in_hbm(hidden_in), in_hbm(attn_gain[None, :]), in_hbm(segment_ids), in_hbm(attn_routes.T))
    chunks = gather_head(own)
    gu_x = send_xy(gu, WX)
    down_y = send_xy(down, WY)
    gu_y = send_xy(gu, WY)
    down_x = send_xy(down, WX)
    gu_xr = gu_x.reshape(2 * HID, D)[:CUT]
    gu_yr = gu_y.reshape(2 * HID, D)[CUT:]
    gu_d = send_xy(gu_xr, WY)
    gu_e = send_xy(gu_yr, WX)
    down_d = send_xy(down_y, WX)

    half = HD // 2
    inverse = ROPE_BASE ** (-jnp.arange(half, dtype=F32) / half)
    angles = jnp.arange(SEQ, dtype=F32)[:, None] * jnp.concatenate([inverse, inverse])[None, :]
    cosine, sine = jnp.cos(angles), jnp.sin(angles)
    keep, send = attention(
        chunks, in_hbm(attn_router.T), cosine, sine,
        in_hbm(w_query), in_hbm(w_key), in_hbm(w_value), in_hbm(w_out),
    )
    got = send_h(send, HC)
    pass_a = (keep[128:].astype(F32) + got[128:].astype(F32)).astype(BF)
    got_a = send_h(pass_a, HA)
    held = keep[64:128].astype(F32) + got[64:128].astype(F32) + got_a[64:].astype(F32)
    got_b = send_h(held.astype(BF), HB)
    residual, rows = settle(hidden_in, keep, got, got_a, got_b, ffn_gain[None, :], ffn_routes.T)
    arrived = lax.all_to_all(rows.reshape(8, SLOTS, D), "head", split_axis=0, concat_axis=0, tiled=True)
    high, low = weigh(residual, ffn_gain[None, :], ffn_router.T, ffn_routes.T)
    x_own = arrived.reshape(8 * SLOTS, D)
    weights = pack((in_hbm(gu), in_hbm(gu_x), in_hbm(gu_y), gu_d, gu_e), (in_hbm(down), down_x, down_y, down_d))
    x_d = send_xy(x_own, TXY)
    x_x = send_xy(x_own, TX)
    x_y = send_xy(x_own, TY)
    (part_d,) = experts([x_d], weights)
    got_d = send_xy(part_d, TXY)
    part_x, part_y = experts([x_x, x_y], weights)
    got_x = send_xy(part_x, TX)
    got_y = send_xy(part_y, TY)
    (part,) = experts([x_own], weights)
    rows = part.astype(F32) + got_d.astype(F32) + got_x.astype(F32) + got_y.astype(F32)
    rows = rows.astype(BF).reshape(8, SLOTS, D)
    returned = lax.all_to_all(rows, "head", split_axis=0, concat_axis=0, tiled=True)
    return finish(residual, high, low, returned.reshape(8 * SLOTS, D))


def solution(mesh):
    return jax.shard_map(
        per_device,
        mesh=mesh,
        in_specs=(
            P(("req", "head"), None),
            P("req", "head"),
            P(("req", "head"), None),
            P(("req", "head"), None),
            P(),
            P(),
            P(None, None, "head"),
            P(None, "head"),
            P(None, "head"),
            P(None, "head", None),
            P(),
            P(),
            P("head", None, None, "req"),
            P("head", "req", None),
        ),
        out_specs=P(("req", "head"), None),
        check_vma=False,
    )
```
